256 devices in a mesh: leaf: 32 (over x, z), panel: 8 (over y, core).
Axes of the slice: x: 4, y: 4, z: 8, core: 2. Of those that a mesh axis runs over, the one named last changes fastest.
Arguments:
- child_cost: float32 [512, 512, 512], P('leaf', 'panel'), as said below
- panel: bfloat16 [64, 4096, 512], P('leaf', 'panel'), may hold values from -0.25 to 0.25
- section_weight: float32 [64, 512], P('leaf'), may hold values from 0.5 to 4
- parent_slots: int32 [64, 8], replicated, may hold values from 0 to 511, as said below
- child_count: int32 [64], replicated, may hold values from 1 to 8, as said below
Outputs:
- cost_to_go: float32 [64, 384, 384], P('leaf', 'panel')
- gain: float32 [64, 128, 384], P('leaf', 'panel')
The draws below stay inside these ranges and needn't reach their ends.
Inputs may be any that keep to these rules, and one draw needn't show every extreme that they name: `parent_slots`: child number c is stored at leaf index c // 16. Only the first child_count[p] slots of parent p are used; the others hold child numbers that are ignored. No child is named twice. Each aligned run of 2 slots of a parent names children stored at one leaf index. The parents of one owner (rows o * 2 to (o + 1) * 2 - 1) name at most 2 children stored at any one leaf index, and this bound is reached by used slots in every draw. `child_count`: some parent has 8 used slots and some has one. `child_cost`: each child's matrix is symmetric positive definite.
All inputs are finite; a program needn't handle non-finite values.
Results may differ from the reference program's by a relative error of at most 0.00035.
Values may be sent and summed in bfloat16 or wider, within the bound.
A program may use at most 128 MiB of HBM per device.

```python
import math
import jax
import jax.numpy as jnp
from jax import lax

NS = 512
NZ = 512
NU = 128
SLOTS = 8
PAR_DEV = 2
CAP = 2
CH_DEV = 16
PARENTS = 64
CHILDREN = 512


def draw_child_cost(key, part):
    child_keys = jax.random.split(jax.random.fold_in(key, 3), CHILDREN)

    def make_one(child_key):
        key_fac, key_diag = jax.random.split(child_key, 2)
        factor = jax.random.normal(key_fac, (NS, 2 * NS), jnp.float32)
        diagonal = jnp.exp(jax.random.uniform(key_diag, (NS,), jnp.float32, math.log(0.3), 0.0))
        gram = jnp.dot(factor, factor.T, precision=lax.Precision.HIGHEST) / (2.0 * NS)
        gram = 0.5 * (gram + gram.T)
        return gram + jnp.diag(diagonal)
    return lax.map(make_one, child_keys)


def draw_parent_slots(key, part):
    owners = PARENTS // PAR_DEV
    groups = PAR_DEV * SLOTS // CAP
    key_shift, key_order = jax.random.split(jax.random.fold_in(key, 11))
    shuffled = jax.random.permutation(key_shift, owners)
    far_offset = owners // 2
    near_offset = owners - 1
    priority = jnp.where(shuffled == far_offset, -2, jnp.where(shuffled == near_offset, -1, jnp.arange(owners)))
    offsets = shuffled[jnp.argsort(priority)][:groups]
    owner_index = jnp.arange(owners)[:, None]
    source = (owner_index + offsets[None, :]) % owners
    order_keys = jax.random.split(key_order, owners)
    local_order = jax.vmap(lambda k: jax.random.permutation(k, CH_DEV))(order_keys)
    run_start = (jnp.arange(groups) * CAP)[None, :, None]
    local_slot = run_start + jnp.arange(CAP)[None, None, :]
    child_ids = source[:, :, None] * CH_DEV + local_order[source[:, :, None], local_slot]
    return child_ids.reshape(PARENTS, SLOTS).astype(jnp.int32)


def draw_child_count(key, part):
    key_base, key_full, key_one = jax.random.split(jax.random.fold_in(key, 5), 3)
    counts = jax.random.randint(key_base, (PARENTS,), 1, SLOTS + 1)
    full_at = jax.random.randint(key_full, (), 0, PARENTS)
    single_at = (full_at + 1 + jax.random.randint(key_one, (), 0, PARENTS - 1)) % PARENTS
    index_row = jnp.arange(PARENTS)
    counts = jnp.where(index_row == full_at, SLOTS, counts)
    counts = jnp.where(index_row == single_at, 1, counts)
    return counts.astype(jnp.int32)


def steps_of(key, shape, shards, low, top_value):
    level, own = 1.0, jax.random.fold_in(key, 6)
    for axis_at, shards_of in shards:
        steps = jnp.exp(jax.random.uniform(jax.random.fold_in(own, axis_at), (shards_of,), jnp.float32, low / len(shards), top_value / len(shards)))
        level = level * jnp.repeat(steps, shape[axis_at] // shards_of).reshape([-1 if axis == axis_at else 1 for axis in range(len(shape))])
    return level


def normal_values(rng, shape, deviation, bound, pieces=(), dtype=jnp.bfloat16):
    array = jax.random.normal(rng, shape, jnp.float32) * deviation
    if len(pieces) > 0:
        array = steps_of(rng, shape, pieces, -0.22, 0.18) * array
    return jnp.clip(array, min=-bound, max=bound).astype(dtype)


def setup_inputs(seed: int = 0) -> dict:
    key_list = jax.random.split(jax.random.key(seed), 6)
    child_cost = draw_child_cost(jax.random.fold_in(key_list[5], 71), 0)
    panel = normal_values(key_list[1], (PARENTS, SLOTS * NS, NZ), NZ ** -0.5, 0.25, ((0, 32), (1, 8)))
    section_weight = jnp.clip(jnp.exp(math.log(4.0) - 2.0794415 * jax.random.uniform(key_list[2], (PARENTS, NZ), jnp.float32) ** steps_of(key_list[2], (PARENTS, NZ), ((0, 32),), -0.2, 0.2)), 0.5, 4.0)
    parent_slots = draw_parent_slots(jax.random.fold_in(key_list[5], 71), 0)
    child_count = draw_child_count(jax.random.fold_in(key_list[5], 71), 0)
    return {"child_cost": child_cost, "panel": panel, "section_weight": section_weight, "parent_slots": parent_slots, "child_count": child_count}


def reference(child_cost, panel, section_weight, parent_slots, child_count):

    def per_parent(item):
        blocks, weights, slot_ids, count = item
        chosen = jnp.take(child_cost, slot_ids, axis=0)
        live_mask = (jnp.arange(SLOTS) < count).astype(jnp.float32)
        chosen = chosen * live_mask[:, None, None]
        panel_blocks = blocks.reshape(SLOTS, NS, NZ).astype(jnp.float32)
        projected = jnp.einsum('krs,ksz->krz', chosen, panel_blocks, precision=lax.Precision.HIGHEST)
        curvature = jnp.einsum('krz,kry->zy', panel_blocks, projected, precision=lax.Precision.HIGHEST)
        return curvature + jnp.diag(weights)
    curvature = lax.map(per_parent, (panel, section_weight, parent_slots, child_count))
    factor = jnp.linalg.cholesky(curvature)
    ctrl_block = factor[:, :NU, :NU]
    cross_block = factor[:, NU:, :NU]
    state_block = factor[:, NU:, NU:]
    cost_to_go = jnp.einsum('pab,pcb->pac', state_block, state_block, precision=lax.Precision.HIGHEST)
    gain = -lax.linalg.triangular_solve(ctrl_block, jnp.swapaxes(cross_block, 1, 2), left_side=True, lower=True, transpose_a=True)
    return (cost_to_go, gain)
```

```python
import jax
import jax.numpy as jnp
from jax import lax
from jax.sharding import PartitionSpec as P

NU = 128
HI = lax.Precision.HIGHEST


def split(x):
    top = lax.reduce_precision(x, 8, 7)
    return top.astype(jnp.bfloat16), (x - top).astype(jnp.bfloat16)


def per_device(child_cost, panel, section_weight, parent_slots, child_count):
    leaves = lax.axis_size("leaf")
    panels = lax.axis_size("panel")
    own_leaf = lax.axis_index("leaf")
    own_panel = lax.axis_index("panel")
    par_dev, _, decision = panel.shape
    slot_count = parent_slots.shape[1]
    stored, row_block, state_order = child_cost.shape
    positions = par_dev * slot_count
    top = jnp.maximum(jnp.max(jnp.abs(child_cost), axis=(1, 2)), 1e-30)
    coded = (child_cost * (30000.0 / top)[:, None, None]).astype(jnp.float16)
    scale_all = lax.all_gather(top * (1.0 / 30000.0), "leaf", axis=0, tiled=True)
    gathered = lax.all_gather(panel, "panel", axis=1, tiled=True)
    rg, cb = row_block // 8, state_order // 128
    pieces = coded.reshape(stored, rg, 8, cb, 128).transpose(1, 3, 0, 2, 4)
    pieces = pieces.reshape(leaves, stored, 8, 128)
    held = lax.all_to_all(pieces, "leaf", split_axis=0, concat_axis=0, tiled=True)
    ordered = jnp.take(held.reshape(leaves * stored, 8, 128), parent_slots.reshape(-1), axis=0)
    ordered = ordered.reshape(leaves, positions, 8, 128)
    mine = lax.all_to_all(ordered, "leaf", split_axis=0, concat_axis=0, tiled=True)
    rows = mine.reshape(rg, cb, positions, 8, 128).transpose(2, 0, 3, 1, 4)
    rows = rows.reshape(par_dev, slot_count, row_block, state_order).astype(jnp.float32)
    my_ids = lax.dynamic_slice_in_dim(parent_slots, own_leaf * par_dev, par_dev, 0)
    my_count = lax.dynamic_slice_in_dim(child_count, own_leaf * par_dev, par_dev, 0)
    live = jnp.arange(slot_count)[None, :] < my_count[:, None]
    scale = jnp.where(live, jnp.take(scale_all, my_ids, axis=0), 0.0)
    hi, lo = split(rows)
    slot_rows = gathered.reshape(par_dev, slot_count, state_order, decision)
    both = jnp.concatenate([hi, lo], axis=2)
    prod = jnp.einsum("pkrs,pksz->pkrz", both, slot_rows, preferred_element_type=jnp.float32)
    prod = (prod[:, :, :row_block] + prod[:, :, row_block:]) * scale[:, :, None, None]
    own_rows = lax.dynamic_slice_in_dim(slot_rows, own_panel * row_block, row_block, 2)
    phi, plo = split(prod)
    partial_sum = jnp.einsum(
        "pkaz,pkay->pzy",
        jnp.concatenate([own_rows, own_rows], axis=2),
        jnp.concatenate([phi, plo], axis=2),
        preferred_element_type=jnp.float32,
    )
    curvature = lax.psum(partial_sum, "panel") + jax.vmap(jnp.diag)(section_weight)
    ctrl = curvature[:, :NU, :NU]
    cross = curvature[:, :NU, NU:]
    factor = jnp.linalg.cholesky(ctrl)
    w = lax.linalg.triangular_solve(factor, cross, left_side=True, lower=True)
    gain_full = -lax.linalg.triangular_solve(
        factor, w, left_side=True, lower=True, transpose_a=True
    )
    rows_out = (decision - NU) // panels
    state_rows = lax.dynamic_slice_in_dim(curvature, NU + own_panel * rows_out, rows_out, 1)
    w_rows = lax.dynamic_slice_in_dim(w, own_panel * rows_out, rows_out, 2)
    cost_rows = state_rows[:, :, NU:] - jnp.einsum("pba,pbc->pac", w_rows, w, precision=HI)
    gain_rows = lax.dynamic_slice_in_dim(gain_full, own_panel * (NU // panels), NU // panels, 1)
    return (cost_rows, gain_rows)


def solution(mesh):
    in_specs = (P("leaf", "panel", None), P("leaf", "panel", None), P("leaf", None), P(), P())
    out_specs = (P("leaf", "panel", None), P("leaf", "panel", None))
    return jax.shard_map(
        per_device, mesh=mesh, in_specs=in_specs, out_specs=out_specs, check_vma=False
    )
```

```python
import functools

import jax
import jax.numpy as jnp
from jax import lax
from jax.experimental import pallas as pl
from jax.experimental.pallas import tpu as pltpu
from jax.sharding import PartitionSpec as P

NU = 128
HI = lax.Precision.HIGHEST


def split(x):
    top = lax.reduce_precision(x, 8, 7)
    return top.astype(jnp.bfloat16), (x - top).astype(jnp.bfloat16)


def sweep(blocks):
    lane = lax.broadcasted_iota(jnp.int32, (8, 128), 1)
    sub = lax.broadcasted_iota(jnp.int32, (8, 128), 0)

    def body(_, carry):
        out = []
        for mat in carry:
            top = mat[0]
            for j in range(8):
                inv = 1.0 / top[j : j + 1, j : j + 1]
                row = jnp.where(lane[:1] == j, inv, top[j : j + 1, :] * inv)
                rest = jnp.where(lane == j, 0.0, top) - top[:, j : j + 1] * row
                top = jnp.where(sub == j, row, rest)
            moved = []
            for blk in mat[1:]:
                new = jnp.where(lane < 8, 0.0, blk)
                for j in range(8):
                    new = new - blk[:, j : j + 1] * top[j : j + 1, :]
                moved.append(pltpu.roll(new, 120, 1))
            moved.append(pltpu.roll(top, 120, 1))
            out.append(tuple(moved))
        return tuple(out)

    return lax.fori_loop(0, 16, body, blocks)


def finish_kernel(panels, h1_ref, h22_ref, weight_ref, cost_ref, gain_ref, inv_ref, x_ref, z_ref):
    own = lax.axis_index("panel")
    par_dev = weight_ref.shape[0]
    gain_rows, cost_rows = gain_ref.shape[1], cost_ref.shape[1]
    lane = lax.broadcasted_iota(jnp.int32, (8, 128), 1)
    sub = lax.broadcasted_iota(jnp.int32, (8, 128), 0)
    mats = []
    for p in range(par_dev):
        blocks = []
        for b in range(NU // 8):
            at = b * 8
            blk = h1_ref[at // gain_rows, p, at % gain_rows : at % gain_rows + 8, :NU]
            blocks.append(blk + jnp.where(lane == sub + at, weight_ref[p : p + 1, :NU], 0.0))
        mats.append(tuple(blocks))
    mats = sweep(tuple(mats))
    at_cost = pl.multiple_of(own * cost_rows, 8)
    at_gain = pl.multiple_of(own * gain_rows, 8)
    width = cost_ref.shape[2]
    on_diag = lax.broadcasted_iota(jnp.int32, (cost_rows, width), 1) == (
        lax.broadcasted_iota(jnp.int32, (cost_rows, width), 0) + at_cost
    )
    for p in range(par_dev):
        for b in range(NU // 8):
            inv_ref[b * 8 : b * 8 + 8, :] = mats[p][b]
        cross = jnp.concatenate([h1_ref[q, p, :, NU:] for q in range(panels)], axis=0)
        x_ref[...] = jnp.dot(inv_ref[...], cross, precision=HI, preferred_element_type=jnp.float32)
        z_ref[...] = lax.dot_general(
            cross, x_ref[...], (((0,), (0,)), ((), ())), precision=HI,
            preferred_element_type=jnp.float32,
        )
        gain_ref[p] = -x_ref[pl.ds(at_gain, gain_rows), :]
        cost_ref[p] = (
            h22_ref[p]
            + jnp.where(on_diag, weight_ref[p : p + 1, NU:], 0.0)
            - z_ref[pl.ds(at_cost, cost_rows), :]
        )


def finish(h1, h22, section_weight, panels):
    par_dev, cost_rows, width = h22.shape
    return pl.pallas_call(
        functools.partial(finish_kernel, panels),
        out_shape=(
            jax.ShapeDtypeStruct((par_dev, cost_rows, width), jnp.float32),
            jax.ShapeDtypeStruct((par_dev, NU // panels, width), jnp.float32),
        ),
        in_specs=[pl.BlockSpec(memory_space=pltpu.VMEM)] * 3,
        out_specs=(pl.BlockSpec(memory_space=pltpu.VMEM),) * 2,
        scratch_shapes=[
            pltpu.VMEM((NU, NU), jnp.float32),
            pltpu.VMEM((NU, width), jnp.float32),
            pltpu.VMEM((width, width), jnp.float32),
        ],
        compiler_params=pltpu.CompilerParams(vmem_limit_bytes=32 << 20),
        name="finish",
    )(h1, h22, section_weight)


def reduce_kernel(
    panels, part_ref, h1_ref, h22_ref, mate1, mate2, acc1, acc2, in1, in2,
    m1s, m1r, m2s, m2r, d1s, d1r, d2s, d2r, gs, gr,
):
    own = lax.axis_index("panel")
    chips = panels // 2
    chip, core = own // 2, own % 2
    mate = 2 * chip + 1 - core
    n1, n2 = h1_ref.shape[2], h22_ref.shape[1]

    def send(src, dst, ssem, rsem, to):
        return pltpu.make_async_remote_copy(
            src_ref=src, dst_ref=dst, send_sem=ssem, recv_sem=rsem,
            device_id={"panel": to}, device_id_type=pl.DeviceIdType.MESH,
        )

    barrier = pltpu.get_barrier_semaphore()
    for j in range(1, panels):
        pl.semaphore_signal(
            barrier, inc=1, device_id={"panel": lax.rem(own + j, panels)},
            device_id_type=pl.DeviceIdType.MESH,
        )
    pl.semaphore_wait(barrier, panels - 1)

    def rows1(t, c):
        return pl.ds(pl.multiple_of((2 * t + c) * n1, 8), n1)

    def rows2(t, c):
        return pl.ds(pl.multiple_of(NU + (2 * t + c) * n2, 8), n2)

    first = [
        send(part_ref.at[:, rows1(t, 1 - core), :], mate1.at[t], m1s.at[t], m1r.at[t], mate)
        for t in range(chips)
    ]
    second = [
        send(part_ref.at[:, rows2(t, 1 - core), NU:], mate2.at[t], m2s.at[t], m2r.at[t], mate)
        for t in range(chips)
    ]
    for copy in first + second:
        copy.start()
    others = [lax.rem(chip + j, chips) for j in range(1, chips)]

    def spread(acc, land, ssem, rsem):
        return [
            send(acc.at[o], land.at[j], ssem.at[j], rsem.at[j], 2 * o + core)
            for j, o in enumerate(others)
        ]

    for t in range(chips):
        first[t].wait_recv()
        acc1[t] = part_ref[:, rows1(t, core), :] + mate1[t]
    out1 = spread(acc1, in1, d1s, d1r)
    for copy in out1:
        copy.start()
    for t in range(chips):
        second[t].wait_recv()
        acc2[t] = part_ref[:, rows2(t, core), NU:] + mate2[t]
    out2 = spread(acc2, in2, d2s, d2r)
    for copy in out2:
        copy.start()
    for copy in out1:
        copy.wait_recv()
    total = acc1[chip]
    for j in range(chips - 1):
        total = total + in1[j]
    h1_ref[own] = total
    share = [
        send(h1_ref.at[own], h1_ref.at[own], gs.at[j - 1], gr.at[j - 1], lax.rem(own + j, panels))
        for j in range(1, panels)
    ]
    for copy in share:
        copy.start()
    for copy in out2:
        copy.wait_recv()
    total = acc2[chip]
    for j in range(chips - 1):
        total = total + in2[j]
    h22_ref[...] = total
    for j in range(1, panels):
        source = lax.rem(own + panels - j, panels)
        send(
            h1_ref.at[source], h1_ref.at[source], gs.at[j - 1], gr.at[j - 1],
            lax.rem(own + j, panels),
        ).wait_recv()
    for copy in first + second + out1 + out2 + share:
        copy.wait_send()


def reduce(part, panels):
    par_dev, order, _ = part.shape
    chips = panels // 2
    n1, n2 = NU // panels, (order - NU) // panels
    one = (par_dev, n1, order)
    two = (par_dev, n2, order - NU)
    vmem = pl.BlockSpec(memory_space=pltpu.VMEM)
    dma = pltpu.SemaphoreType.DMA
    return pl.pallas_call(
        functools.partial(reduce_kernel, panels),
        out_shape=(
            jax.ShapeDtypeStruct((panels,) + one, jnp.float32),
            jax.ShapeDtypeStruct(two, jnp.float32),
        ),
        in_specs=[vmem],
        out_specs=(vmem, vmem),
        scratch_shapes=[
            pltpu.VMEM((chips,) + one, jnp.float32),
            pltpu.VMEM((chips,) + two, jnp.float32),
            pltpu.VMEM((chips,) + one, jnp.float32),
            pltpu.VMEM((chips,) + two, jnp.float32),
            pltpu.VMEM((chips - 1,) + one, jnp.float32),
            pltpu.VMEM((chips - 1,) + two, jnp.float32),
        ]
        + [dma((chips,))] * 4
        + [dma((chips - 1,))] * 4
        + [dma((panels - 1,))] * 2,
        compiler_params=pltpu.CompilerParams(
            collective_id=0, has_side_effects=True, vmem_limit_bytes=32 << 20
        ),
        name="reduce",
    )(part)


def per_device(child_cost, panel, section_weight, parent_slots, child_count):
    leaves = lax.axis_size("leaf")
    panels = lax.axis_size("panel")
    own_leaf = lax.axis_index("leaf")
    own_panel = lax.axis_index("panel")
    par_dev, _, decision = panel.shape
    slot_count = parent_slots.shape[1]
    stored, row_block, state_order = child_cost.shape
    positions = par_dev * slot_count
    top = jnp.maximum(jnp.max(jnp.abs(child_cost), axis=(1, 2)), 1e-30)
    coded = (child_cost * (30000.0 / top)[:, None, None]).astype(jnp.float16)
    scale_all = lax.all_gather(top * (1.0 / 30000.0), "leaf", axis=0, tiled=True)
    gathered = lax.all_gather(panel, "panel", axis=1, tiled=True)
    rg, cb = row_block // 8, state_order // 128
    pieces = coded.reshape(stored, rg, 8, cb, 128).transpose(1, 3, 0, 2, 4)
    pieces = pieces.reshape(leaves, stored, 8, 128)
    held = lax.all_to_all(pieces, "leaf", split_axis=0, concat_axis=0, tiled=True)
    ordered = jnp.take(held.reshape(leaves * stored, 8, 128), parent_slots.reshape(-1), axis=0)
    ordered = ordered.reshape(leaves, positions, 8, 128)
    mine = lax.all_to_all(ordered, "leaf", split_axis=0, concat_axis=0, tiled=True)
    rows = mine.reshape(rg, cb, positions, 8, 128).transpose(2, 0, 3, 1, 4)
    rows = rows.reshape(par_dev, slot_count, row_block, state_order).astype(jnp.float32)
    my_ids = lax.dynamic_slice_in_dim(parent_slots, own_leaf * par_dev, par_dev, 0)
    my_count = lax.dynamic_slice_in_dim(child_count, own_leaf * par_dev, par_dev, 0)
    live = jnp.arange(slot_count)[None, :] < my_count[:, None]
    scale = jnp.where(live, jnp.take(scale_all, my_ids, axis=0), 0.0)
    hi, lo = split(rows)
    slot_rows = gathered.reshape(par_dev, slot_count, state_order, decision)
    both = jnp.concatenate([hi, lo], axis=2)
    prod = jnp.einsum("pkrs,pksz->pkrz", both, slot_rows, preferred_element_type=jnp.float32)
    prod = (prod[:, :, :row_block] + prod[:, :, row_block:]) * scale[:, :, None, None]
    own_rows = lax.dynamic_slice_in_dim(slot_rows, own_panel * row_block, row_block, 2)
    phi, plo = split(prod)
    partial_sum = jnp.einsum(
        "pkaz,pkay->pzy",
        jnp.concatenate([own_rows, own_rows], axis=2),
        jnp.concatenate([phi, plo], axis=2),
        preferred_element_type=jnp.float32,
    )
    h1, h22 = reduce(partial_sum, panels)
    return finish(h1, h22, section_weight, panels)


def solution(mesh):
    in_specs = (P("leaf", "panel", None), P("leaf", "panel", None), P("leaf", None), P(), P())
    out_specs = (P("leaf", "panel", None), P("leaf", "panel", None))
    return jax.shard_map(
        per_device, mesh=mesh, in_specs=in_specs, out_specs=out_specs, check_vma=False
    )
```

```python
import functools

import jax
import jax.numpy as jnp
from jax import lax
from jax.experimental import pallas as pl
from jax.experimental.pallas import tpu as pltpu
from jax.sharding import PartitionSpec as P

NU = 128
HI = lax.Precision.HIGHEST


def split(x):
    top = lax.reduce_precision(x, 8, 7)
    return top.astype(jnp.bfloat16), (x - top).astype(jnp.bfloat16)


def sweep(blocks):
    lane = lax.broadcasted_iota(jnp.int32, (8, 128), 1)
    sub = lax.broadcasted_iota(jnp.int32, (8, 128), 0)

    def body(_, carry):
        out = []
        for mat in carry:
            top = mat[0]
            for j in range(8):
                inv = 1.0 / top[j : j + 1, j : j + 1]
                row = jnp.where(lane[:1] == j, inv, top[j : j + 1, :] * inv)
                rest = jnp.where(lane == j, 0.0, top) - top[:, j : j + 1] * row
                top = jnp.where(sub == j, row, rest)
            moved = []
            for blk in mat[1:]:
                new = jnp.where(lane < 8, 0.0, blk)
                for j in range(8):
                    new = new - blk[:, j : j + 1] * top[j : j + 1, :]
                moved.append(pltpu.roll(new, 120, 1))
            moved.append(pltpu.roll(top, 120, 1))
            out.append(tuple(moved))
        return tuple(out)

    return lax.fori_loop(0, 16, body, blocks)


def finish_kernel(panels, h1_ref, h22_ref, weight_ref, cost_ref, gain_ref, inv_ref, x_ref, z_ref):
    own = lax.axis_index("panel")
    par_dev = weight_ref.shape[0]
    gain_rows, cost_rows = gain_ref.shape[1], cost_ref.shape[1]
    lane = lax.broadcasted_iota(jnp.int32, (8, 128), 1)
    sub = lax.broadcasted_iota(jnp.int32, (8, 128), 0)
    mats = []
    for p in range(par_dev):
        blocks = []
        for b in range(NU // 8):
            at = b * 8
            blk = h1_ref[at // gain_rows, p, at % gain_rows : at % gain_rows + 8, :NU]
            blocks.append(blk + jnp.where(lane == sub + at, weight_ref[p : p + 1, :NU], 0.0))
        mats.append(tuple(blocks))
    mats = sweep(tuple(mats))
    at_cost = pl.multiple_of(own * cost_rows, 8)
    at_gain = pl.multiple_of(own * gain_rows, 8)
    width = cost_ref.shape[2]
    on_diag = lax.broadcasted_iota(jnp.int32, (cost_rows, width), 1) == (
        lax.broadcasted_iota(jnp.int32, (cost_rows, width), 0) + at_cost
    )
    for p in range(par_dev):
        for b in range(NU // 8):
            inv_ref[b * 8 : b * 8 + 8, :] = mats[p][b]
        cross = jnp.concatenate([h1_ref[q, p, :, NU:] for q in range(panels)], axis=0)
        x_ref[...] = jnp.dot(inv_ref[...], cross, precision=HI, preferred_element_type=jnp.float32)
        z_ref[...] = lax.dot_general(
            cross, x_ref[...], (((0,), (0,)), ((), ())), precision=HI,
            preferred_element_type=jnp.float32,
        )
        gain_ref[p] = -x_ref[pl.ds(at_gain, gain_rows), :]
        cost_ref[p] = (
            h22_ref[p]
            + jnp.where(on_diag, weight_ref[p : p + 1, NU:], 0.0)
            - z_ref[pl.ds(at_cost, cost_rows), :]
        )


def finish(h1, h22, section_weight, panels):
    par_dev, cost_rows, width = h22.shape
    return pl.pallas_call(
        functools.partial(finish_kernel, panels),
        out_shape=(
            jax.ShapeDtypeStruct((par_dev, cost_rows, width), jnp.float32),
            jax.ShapeDtypeStruct((par_dev, NU // panels, width), jnp.float32),
        ),
        in_specs=[pl.BlockSpec(memory_space=pltpu.VMEM)] * 3,
        out_specs=(pl.BlockSpec(memory_space=pltpu.VMEM),) * 2,
        scratch_shapes=[
            pltpu.VMEM((NU, NU), jnp.float32),
            pltpu.VMEM((NU, width), jnp.float32),
            pltpu.VMEM((width, width), jnp.float32),
        ],
        compiler_params=pltpu.CompilerParams(vmem_limit_bytes=32 << 20),
        name="finish",
    )(h1, h22, section_weight)


def reduce_kernel(
    panels, part_ref, h1_ref, h22_ref, mate1, mate2, acc1, acc2, in1, in2,
    m1s, m1r, m2s, m2r, d1s, d1r, d2s, d2r, gs, gr,
):
    own = lax.axis_index("panel")
    chips = panels // 2
    chip, core = own // 2, own % 2
    mate = 2 * chip + 1 - core
    n1, n2 = h1_ref.shape[2], h22_ref.shape[1]

    def send(src, dst, ssem, rsem, to):
        return pltpu.make_async_remote_copy(
            src_ref=src, dst_ref=dst, send_sem=ssem, recv_sem=rsem,
            device_id={"panel": to}, device_id_type=pl.DeviceIdType.MESH,
        )

    barrier = pltpu.get_barrier_semaphore()
    for j in range(1, panels):
        pl.semaphore_signal(
            barrier, inc=1, device_id={"panel": lax.rem(own + j, panels)},
            device_id_type=pl.DeviceIdType.MESH,
        )
    pl.semaphore_wait(barrier, panels - 1)

    def rows1(t, c):
        return pl.ds(pl.multiple_of((2 * t + c) * n1, 8), n1)

    def rows2(t, c):
        return pl.ds(pl.multiple_of(NU + (2 * t + c) * n2, 8), n2)

    first = [
        send(part_ref.at[:, rows1(t, 1 - core), :], mate1.at[t], m1s.at[t], m1r.at[t], mate)
        for t in range(chips)
    ]
    second = [
        send(part_ref.at[:, rows2(t, 1 - core), NU:], mate2.at[t], m2s.at[t], m2r.at[t], mate)
        for t in range(chips)
    ]
    for copy in first + second:
        copy.start()
    others = [lax.rem(chip + j, chips) for j in range(1, chips)]

    def spread(acc, land, ssem, rsem):
        return [
            send(acc.at[o], land.at[j], ssem.at[j], rsem.at[j], 2 * o + core)
            for j, o in enumerate(others)
        ]

    for t in range(chips):
        first[t].wait_recv()
        acc1[t] = part_ref[:, rows1(t, core), :] + mate1[t]
    out1 = spread(acc1, in1, d1s, d1r)
    for copy in out1:
        copy.start()
    for t in range(chips):
        second[t].wait_recv()
        acc2[t] = part_ref[:, rows2(t, core), NU:] + mate2[t]
    out2 = spread(acc2, in2, d2s, d2r)
    for copy in out2:
        copy.start()
    for copy in out1:
        copy.wait_recv()
    total = acc1[chip]
    for j in range(chips - 1):
        total = total + in1[j]
    h1_ref[own] = total
    share = [
        send(h1_ref.at[own], h1_ref.at[own], gs.at[j - 1], gr.at[j - 1], lax.rem(own + j, panels))
        for j in range(1, panels)
    ]
    for copy in share:
        copy.start()
    for copy in out2:
        copy.wait_recv()
    total = acc2[chip]
    for j in range(chips - 1):
        total = total + in2[j]
    h22_ref[...] = total
    for j in range(1, panels):
        source = lax.rem(own + panels - j, panels)
        send(
            h1_ref.at[source], h1_ref.at[source], gs.at[j - 1], gr.at[j - 1],
            lax.rem(own + j, panels),
        ).wait_recv()
    for copy in first + second + out1 + out2 + share:
        copy.wait_send()


def reduce(part, panels):
    par_dev, order, _ = part.shape
    chips = panels // 2
    n1, n2 = NU // panels, (order - NU) // panels
    one = (par_dev, n1, order)
    two = (par_dev, n2, order - NU)
    vmem = pl.BlockSpec(memory_space=pltpu.VMEM)
    dma = pltpu.SemaphoreType.DMA
    return pl.pallas_call(
        functools.partial(reduce_kernel, panels),
        out_shape=(
            jax.ShapeDtypeStruct((panels,) + one, jnp.float32),
            jax.ShapeDtypeStruct(two, jnp.float32),
        ),
        in_specs=[vmem],
        out_specs=(vmem, vmem),
        scratch_shapes=[
            pltpu.VMEM((chips,) + one, jnp.float32),
            pltpu.VMEM((chips,) + two, jnp.float32),
            pltpu.VMEM((chips,) + one, jnp.float32),
            pltpu.VMEM((chips,) + two, jnp.float32),
            pltpu.VMEM((chips - 1,) + one, jnp.float32),
            pltpu.VMEM((chips - 1,) + two, jnp.float32),
        ]
        + [dma((chips,))] * 4
        + [dma((chips - 1,))] * 4
        + [dma((panels - 1,))] * 2,
        compiler_params=pltpu.CompilerParams(
            collective_id=0, has_side_effects=True, vmem_limit_bytes=32 << 20
        ),
        name="reduce",
    )(part)


CODE = 32767.0


def route_kernel(
    leaves, panels, slots_ref, count_ref, child_ref, out_ref,
    send1, held, send2, mine, land, scale_all, scale_out, scale_in,
    as_, ar, bs, br, cs, cr, ds, dr, es, er,
):
    leaf = lax.axis_index("leaf")
    own = lax.axis_index("panel")
    stored, row_block, order = child_ref.shape
    slot_count = slots_ref.shape[1]
    half = row_block // 2
    lane = lax.broadcasted_iota(jnp.int32, (1, 128), 1)

    def offset(j):
        step = (j + 1) // 2
        return step + (leaves - 2 * step) * (1 - lax.rem(j, 2))

    def send(src, dst, ssem, rsem, **to):
        return pltpu.make_async_remote_copy(
            src_ref=src, dst_ref=dst, send_sem=ssem, recv_sem=rsem,
            device_id=to, device_id_type=pl.DeviceIdType.MESH,
        )

    barrier = pltpu.get_barrier_semaphore()

    @pl.loop(1, leaves)
    def _(j):
        pl.semaphore_signal(
            barrier, inc=1, device_id={"leaf": lax.rem(leaf + j, leaves)},
            device_id_type=pl.DeviceIdType.MESH,
        )

    for j in range(1, panels):
        pl.semaphore_signal(
            barrier, inc=1, device_id={"panel": lax.rem(own + j, panels)},
            device_id_type=pl.DeviceIdType.MESH,
        )

    def encode(c, row):
        block = child_ref[c]
        top = jnp.maximum(jnp.max(jnp.abs(block), keepdims=True), 1e-30)
        inv = 1.0 / top
        for b in range(order // 128):
            x = child_ref[c, :, b * 128 : b * 128 + 128] * inv
            size = (jnp.sqrt(jnp.abs(x)) * CODE + 0.5).astype(jnp.int32)
            code = jnp.where(x < 0, -size, size)
            word = code[:half] * 65536 + (code[half:] & 65535)
            for g in range(half // 4):
                send1[b * (half // 4) + g, c] = word[4 * g : 4 * g + 4]
        return jnp.where(lane == c, top * (1.0 / (CODE * CODE)), row)

    scale_all[leaf] = lax.fori_loop(0, stored, encode, jnp.zeros((1, 128), jnp.float32))
    pl.semaphore_wait(barrier, leaves + panels - 2)

    def piece(j, source):
        return send(
            send1.at[lax.rem(leaf + offset(j), leaves)],
            held.at[pl.ds(source * stored, stored)],
            as_.at[j - 1], ar.at[j - 1], leaf=lax.rem(leaf + offset(j), leaves),
        )

    def scales(j, source):
        return send(
            scale_all.at[leaf], scale_all.at[source], bs.at[j - 1], br.at[j - 1],
            leaf=lax.rem(leaf + offset(j), leaves),
        )

    def source_of(j):
        return lax.rem(leaf + leaves - offset(j), leaves)

    @pl.loop(1, leaves)
    def _(j):
        piece(j, leaf).start()
        scales(j, leaf).start()

    held[pl.ds(leaf * stored, stored)] = send1[leaf]

    @pl.loop(1, leaves)
    def _(j):
        scales(j, source_of(j)).wait_recv()
        piece(j, source_of(j)).wait_recv()

    par_dev = send2.shape[0]

    def parcel(p, j, source):
        to = lax.rem(leaf + offset(j), leaves)
        return send(
            send2.at[p, to], mine.at[p, source], cs.at[p, j - 1], cr.at[p, j - 1], leaf=to
        )

    def collect(p, d):
        for k in range(slot_count):
            send2[p, d, k] = held[slots_ref[d * par_dev + p, k]]

    for p in range(par_dev):

        @pl.loop(1, leaves)
        def _(j):
            collect(p, lax.rem(leaf + offset(j), leaves))
            parcel(p, j, leaf).start()

        collect(p, leaf)
        mine[p, leaf] = send2[p, leaf]

    for k in range(slot_count):
        row = jnp.zeros((1, 128), jnp.float32)
        for p in range(par_dev):
            parent = leaf * par_dev + p
            child = slots_ref[parent, k]
            value = jnp.sum(
                jnp.where(lane == lax.rem(child, stored), scale_all[child // stored], 0.0),
                axis=1, keepdims=True,
            )
            value = jnp.where(k < count_ref[parent], value, 0.0)
            row = jnp.where(lane == p, value, row)
        scale_out[k] = row

    def tell(j, source):
        to = lax.rem(own + j, panels)
        return send(
            scale_out.at[to], scale_in.at[source], ds.at[j - 1], dr.at[j - 1], panel=to
        )

    def slot(p, j, source):
        to = lax.rem(own + j, panels)
        return send(
            mine.at[p, :, to], land.at[p, source], es.at[p, j - 1], er.at[p, j - 1], panel=to
        )

    def from_of(j):
        return lax.rem(own + panels - j, panels)

    for j in range(1, panels):
        tell(j, own).start()
    scale_in[own] = scale_out[own]
    for p in range(par_dev):

        @pl.loop(1, leaves)
        def _(j):
            parcel(p, j, source_of(j)).wait_recv()

        for j in range(1, panels):
            slot(p, j, own).start()
        land[p, own] = mine[p, :, own]

    for j in range(1, panels):
        tell(j, from_of(j)).wait_recv()

    def decode(p, q):
        scale = scale_in[q][:, p : p + 1]
        for b in range(order // 128):
            at = b * (half // 4)
            word = jnp.concatenate([land[p, q, at + g] for g in range(half // 4)], axis=0)
            for n, code in enumerate((word >> 16, (word << 16) >> 16)):
                v = code.astype(jnp.float32)
                v = v * jnp.abs(v) * scale
                hi = v.astype(jnp.bfloat16)
                lo = (v - hi.astype(jnp.float32)).astype(jnp.bfloat16)
                rows = pl.ds(pl.multiple_of(q * row_block + n * half, half), half)
                low_rows = pl.ds(pl.multiple_of(order + q * row_block + n * half, half), half)
                out_ref[p, rows, b * 128 : b * 128 + 128] = hi
                out_ref[p, low_rows, b * 128 : b * 128 + 128] = lo

    for p in range(par_dev):
        for j in range(1, panels):
            slot(p, j, from_of(j)).wait_recv()

        @pl.loop(0, panels)
        def _(q):
            decode(p, q)

    @pl.loop(1, leaves)
    def _(j):
        piece(j, leaf).wait_send()
        scales(j, leaf).wait_send()
        for p in range(par_dev):
            parcel(p, j, leaf).wait_send()

    for j in range(1, panels):
        tell(j, own).wait_send()
        for p in range(par_dev):
            slot(p, j, own).wait_send()


def route(child_cost, parent_slots, child_count, leaves, panels):
    stored, row_block, order = child_cost.shape
    parents, slot_count = parent_slots.shape
    par_dev = parents // leaves
    piece = (row_block // 2 * order // 128 // leaves, 128)
    vmem = pl.BlockSpec(memory_space=pltpu.VMEM)
    smem = pl.BlockSpec(memory_space=pltpu.SMEM)
    dma = pltpu.SemaphoreType.DMA
    word = lambda *shape: pltpu.VMEM(shape + piece, jnp.int32)
    return pl.pallas_call(
        functools.partial(route_kernel, leaves, panels),
        out_shape=jax.ShapeDtypeStruct((par_dev, 2 * order, order), jnp.bfloat16),
        in_specs=[smem, smem, vmem],
        out_specs=vmem,
        scratch_shapes=[
            word(leaves, stored),
            word(leaves * stored),
            word(par_dev, leaves, slot_count),
            word(par_dev, leaves, slot_count),
            word(par_dev, panels, leaves),
            pltpu.VMEM((leaves, 1, 128), jnp.float32),
            pltpu.VMEM((slot_count, 1, 128), jnp.float32),
            pltpu.VMEM((panels, 1, 128), jnp.float32),
        ]
        + [dma((leaves - 1,))] * 4
        + [dma((par_dev, leaves - 1))] * 2
        + [dma((panels - 1,))] * 2
        + [dma((par_dev, panels - 1))] * 2,
        compiler_params=pltpu.CompilerParams(
            collective_id=1, has_side_effects=True, vmem_limit_bytes=40 << 20
        ),
        name="route",
    )(parent_slots, child_count, child_cost)


def per_device(child_cost, panel, section_weight, parent_slots, child_count):
    leaves = lax.axis_size("leaf")
    panels = lax.axis_size("panel")
    order = child_cost.shape[2]
    both = route(child_cost, parent_slots, child_count, leaves, panels)
    prod = jnp.einsum("prs,psz->prz", both, panel, preferred_element_type=jnp.float32)
    hi, lo = split(prod[:, :order] + prod[:, order:])
    partial_sum = jnp.einsum(
        "paz,pay->pzy",
        jnp.concatenate([panel, panel], axis=1),
        jnp.concatenate([hi, lo], axis=1),
        preferred_element_type=jnp.float32,
    )
    h1, h22 = reduce(partial_sum, panels)
    return finish(h1, h22, section_weight, panels)


def solution(mesh):
    in_specs = (P("leaf", "panel", None), P("leaf", "panel", None), P("leaf", None), P(), P())
    out_specs = (P("leaf", "panel", None), P("leaf", "panel", None))
    return jax.shard_map(
        per_device, mesh=mesh, in_specs=in_specs, out_specs=out_specs, check_vma=False
    )
```

```python
import functools

import jax
import jax.numpy as jnp
from jax import lax
from jax.experimental import pallas as pl
from jax.experimental.pallas import tpu as pltpu
from jax.sharding import PartitionSpec as P

NU = 128
HI = lax.Precision.HIGHEST


def split(x):
    top = lax.reduce_precision(x, 8, 7)
    return top.astype(jnp.bfloat16), (x - top).astype(jnp.bfloat16)


def sweep(blocks):
    lane = lax.broadcasted_iota(jnp.int32, (8, 128), 1)
    sub = lax.broadcasted_iota(jnp.int32, (8, 128), 0)

    def body(_, carry):
        out = []
        for mat in carry:
            top = mat[0]
            for j in range(8):
                inv = 1.0 / top[j : j + 1, j : j + 1]
                row = jnp.where(lane[:1] == j, inv, top[j : j + 1, :] * inv)
                rest = jnp.where(lane == j, 0.0, top) - top[:, j : j + 1] * row
                top = jnp.where(sub == j, row, rest)
            moved = []
            for blk in mat[1:]:
                new = jnp.where(lane < 8, 0.0, blk)
                for j in range(8):
                    new = new - blk[:, j : j + 1] * top[j : j + 1, :]
                moved.append(pltpu.roll(new, 120, 1))
            moved.append(pltpu.roll(top, 120, 1))
            out.append(tuple(moved))
        return tuple(out)

    return lax.fori_loop(0, 16, body, blocks)


def finish_kernel(panels, h1_ref, h22_ref, weight_ref, cost_ref, gain_ref, inv_ref, x_ref, z_ref):
    own = lax.axis_index("panel")
    par_dev = weight_ref.shape[0]
    gain_rows, cost_rows = gain_ref.shape[1], cost_ref.shape[1]
    lane = lax.broadcasted_iota(jnp.int32, (8, 128), 1)
    sub = lax.broadcasted_iota(jnp.int32, (8, 128), 0)
    mats = []
    for p in range(par_dev):
        blocks = []
        for b in range(NU // 8):
            at = b * 8
            blk = h1_ref[at // gain_rows, p, at % gain_rows : at % gain_rows + 8, :NU]
            blocks.append(blk + jnp.where(lane == sub + at, weight_ref[p : p + 1, :NU], 0.0))
        mats.append(tuple(blocks))
    mats = sweep(tuple(mats))
    at_cost = pl.multiple_of(own * cost_rows, 8)
    at_gain = pl.multiple_of(own * gain_rows, 8)
    width = cost_ref.shape[2]
    on_diag = lax.broadcasted_iota(jnp.int32, (cost_rows, width), 1) == (
        lax.broadcasted_iota(jnp.int32, (cost_rows, width), 0) + at_cost
    )
    for p in range(par_dev):
        for b in range(NU // 8):
            inv_ref[b * 8 : b * 8 + 8, :] = mats[p][b]
        cross = jnp.concatenate([h1_ref[q, p, :, NU:] for q in range(panels)], axis=0)
        x_ref[...] = jnp.dot(inv_ref[...], cross, precision=HI, preferred_element_type=jnp.float32)
        z_ref[...] = lax.dot_general(
            cross, x_ref[...], (((0,), (0,)), ((), ())), precision=HI,
            preferred_element_type=jnp.float32,
        )
        gain_ref[p] = -x_ref[pl.ds(at_gain, gain_rows), :]
        cost_ref[p] = (
            h22_ref[p]
            + jnp.where(on_diag, weight_ref[p : p + 1, NU:], 0.0)
            - z_ref[pl.ds(at_cost, cost_rows), :]
        )


def finish(h1, h22, section_weight, panels):
    par_dev, cost_rows, width = h22.shape
    return pl.pallas_call(
        functools.partial(finish_kernel, panels),
        out_shape=(
            jax.ShapeDtypeStruct((par_dev, cost_rows, width), jnp.float32),
            jax.ShapeDtypeStruct((par_dev, NU // panels, width), jnp.float32),
        ),
        in_specs=[pl.BlockSpec(memory_space=pltpu.VMEM)] * 3,
        out_specs=(pl.BlockSpec(memory_space=pltpu.VMEM),) * 2,
        scratch_shapes=[
            pltpu.VMEM((NU, NU), jnp.float32),
            pltpu.VMEM((NU, width), jnp.float32),
            pltpu.VMEM((width, width), jnp.float32),
        ],
        compiler_params=pltpu.CompilerParams(vmem_limit_bytes=32 << 20),
        name="finish",
    )(h1, h22, section_weight)


def reduce_kernel(
    panels, part_ref, h1_ref, h22_ref, mate1, mate2, acc1, acc2, in1, in2,
    m1s, m1r, m2s, m2r, d1s, d1r, d2s, d2r, gs, gr,
):
    own = lax.axis_index("panel")
    chips = panels // 2
    chip, core = own // 2, own % 2
    mate = 2 * chip + 1 - core
    n1, n2 = h1_ref.shape[2], h22_ref.shape[1]

    def send(src, dst, ssem, rsem, to):
        return pltpu.make_async_remote_copy(
            src_ref=src, dst_ref=dst, send_sem=ssem, recv_sem=rsem,
            device_id={"panel": to}, device_id_type=pl.DeviceIdType.MESH,
        )

    barrier = pltpu.get_barrier_semaphore()
    for j in range(1, panels):
        pl.semaphore_signal(
            barrier, inc=1, device_id={"panel": lax.rem(own + j, panels)},
            device_id_type=pl.DeviceIdType.MESH,
        )
    pl.semaphore_wait(barrier, panels - 1)

    def rows1(t, c):
        return pl.ds(pl.multiple_of((2 * t + c) * n1, 8), n1)

    def rows2(t, c):
        return pl.ds(pl.multiple_of(NU + (2 * t + c) * n2, 8), n2)

    first = [
        send(part_ref.at[:, rows1(t, 1 - core), :], mate1.at[t], m1s.at[t], m1r.at[t], mate)
        for t in range(chips)
    ]
    second = [
        send(part_ref.at[:, rows2(t, 1 - core), NU:], mate2.at[t], m2s.at[t], m2r.at[t], mate)
        for t in range(chips)
    ]
    for copy in first + second:
        copy.start()
    others = [lax.rem(chip + j, chips) for j in range(1, chips)]

    def spread(acc, land, ssem, rsem):
        return [
            send(acc.at[o], land.at[j], ssem.at[j], rsem.at[j], 2 * o + core)
            for j, o in enumerate(others)
        ]

    for t in range(chips):
        first[t].wait_recv()
        acc1[t] = part_ref[:, rows1(t, core), :] + mate1[t]
    out1 = spread(acc1, in1, d1s, d1r)
    for copy in out1:
        copy.start()
    for t in range(chips):
        second[t].wait_recv()
        acc2[t] = part_ref[:, rows2(t, core), NU:] + mate2[t]
    out2 = spread(acc2, in2, d2s, d2r)
    for copy in out2:
        copy.start()
    for copy in out1:
        copy.wait_recv()
    total = acc1[chip]
    for j in range(chips - 1):
        total = total + in1[j]
    h1_ref[own] = total
    share = [
        send(h1_ref.at[own], h1_ref.at[own], gs.at[j - 1], gr.at[j - 1], lax.rem(own + j, panels))
        for j in range(1, panels)
    ]
    for copy in share:
        copy.start()
    for copy in out2:
        copy.wait_recv()
    total = acc2[chip]
    for j in range(chips - 1):
        total = total + in2[j]
    h22_ref[...] = total
    for j in range(1, panels):
        source = lax.rem(own + panels - j, panels)
        send(
            h1_ref.at[source], h1_ref.at[source], gs.at[j - 1], gr.at[j - 1],
            lax.rem(own + j, panels),
        ).wait_recv()
    for copy in first + second + out1 + out2 + share:
        copy.wait_send()


def reduce(part, panels):
    par_dev, order, _ = part.shape
    chips = panels // 2
    n1, n2 = NU // panels, (order - NU) // panels
    one = (par_dev, n1, order)
    two = (par_dev, n2, order - NU)
    vmem = pl.BlockSpec(memory_space=pltpu.VMEM)
    dma = pltpu.SemaphoreType.DMA
    return pl.pallas_call(
        functools.partial(reduce_kernel, panels),
        out_shape=(
            jax.ShapeDtypeStruct((panels,) + one, jnp.float32),
            jax.ShapeDtypeStruct(two, jnp.float32),
        ),
        in_specs=[vmem],
        out_specs=(vmem, vmem),
        scratch_shapes=[
            pltpu.VMEM((chips,) + one, jnp.float32),
            pltpu.VMEM((chips,) + two, jnp.float32),
            pltpu.VMEM((chips,) + one, jnp.float32),
            pltpu.VMEM((chips,) + two, jnp.float32),
            pltpu.VMEM((chips - 1,) + one, jnp.float32),
            pltpu.VMEM((chips - 1,) + two, jnp.float32),
        ]
        + [dma((chips,))] * 4
        + [dma((chips - 1,))] * 4
        + [dma((panels - 1,))] * 2,
        compiler_params=pltpu.CompilerParams(
            collective_id=0, has_side_effects=True, vmem_limit_bytes=32 << 20
        ),
        name="reduce",
    )(part)


CODE = 32767.0


def route_kernel(
    leaves, panels, slots_ref, count_ref, child_ref, out_ref,
    send1, held, send2, mine, ready, land, scale_all, scale_out, scale_in,
    as_, ar, bs, br, cs, cr, ds, dr, es, er,
):
    leaf = lax.axis_index("leaf")
    own = lax.axis_index("panel")
    stored, row_block, order = child_ref.shape
    par_dev, _, groups = send2.shape[:3]
    slot_count = slots_ref.shape[1]
    half = row_block // 2
    parts = order // 128
    lane = lax.broadcasted_iota(jnp.int32, (1, 128), 1)
    left = lane < 64
    span = held.shape[0] // leaves
    deep = 3 * half

    def offset(j):
        step = (j + 1) // 2
        return step + (leaves - 2 * step) * (1 - lax.rem(j, 2))

    def send(src, dst, ssem, rsem, **to):
        return pltpu.make_async_remote_copy(
            src_ref=src, dst_ref=dst, send_sem=ssem, recv_sem=rsem,
            device_id=to, device_id_type=pl.DeviceIdType.MESH,
        )

    barrier = pltpu.get_barrier_semaphore()

    @pl.loop(1, leaves)
    def _(j):
        pl.semaphore_signal(
            barrier, inc=1, device_id={"leaf": lax.rem(leaf + j, leaves)},
            device_id_type=pl.DeviceIdType.MESH,
        )

    for j in range(1, panels):
        pl.semaphore_signal(
            barrier, inc=1, device_id={"panel": lax.rem(own + j, panels)},
            device_id_type=pl.DeviceIdType.MESH,
        )

    chip, core = own // 2, own % 2
    upper = chip // (parts // 2)
    side = core + upper - 2 * core * upper

    def encode(c, row):
        cols = [pl.ds(pl.multiple_of(lax.rem(chip + t, parts) * 128, 128), 128) for t in range(3)]
        blocks = [child_ref[c, :, at] for at in cols]
        tops = [jnp.max(jnp.abs(x), keepdims=True) for x in blocks]
        top = jnp.maximum(jnp.maximum(tops[0], tops[1]), jnp.maximum(tops[2], 1e-30))
        inv = 1.0 / top
        words = []
        for x in blocks:
            x = x * inv
            size = (jnp.sqrt(jnp.abs(x)) * CODE + 0.5).astype(jnp.int32)
            code = jnp.where(x < 0, -size, size)
            words.append(code[:half] * 65536 + (code[half:] & 65535))
        for t in range(2):
            send1[pl.ds(t * stored + c, half, stride=span), :] = words[t]
        return words[2], jnp.where(lane == c, top * (1.0 / (CODE * CODE)), row)

    def encode_pair(n, row):
        even, row = encode(2 * n, row)
        odd, row = encode(2 * n + 1, row)
        even = jnp.where(side == 0, even, pltpu.roll(even, 64, 1))
        odd = jnp.where(side == 1, odd, pltpu.roll(odd, 64, 1))
        send1[pl.ds(2 * stored + n, half, stride=span), :] = jnp.where(left, even, odd)
        return row

    scale_all[leaf] = lax.fori_loop(
        0, stored // 2, encode_pair, jnp.zeros((1, 128), jnp.float32)
    )
    pl.semaphore_wait(barrier, leaves + panels - 2)

    def message(i):
        return pl.ds(pl.multiple_of(i * span, 8), span)

    def piece(j, source):
        to = lax.rem(leaf + offset(j), leaves)
        return send(
            send1.at[message(to)], held.at[message(source)],
            as_.at[j - 1], ar.at[j - 1], leaf=to,
        )

    def scales(j, source):
        return send(
            scale_all.at[leaf], scale_all.at[source], bs.at[j - 1], br.at[j - 1],
            leaf=lax.rem(leaf + offset(j), leaves),
        )

    def source_of(j):
        return lax.rem(leaf + leaves - offset(j), leaves)

    @pl.loop(1, leaves)
    def _(j):
        piece(j, leaf).start()
        scales(j, leaf).start()

    held[message(leaf), :] = send1[message(leaf), :]

    @pl.loop(1, leaves)
    def _(j):
        scales(j, source_of(j)).wait_recv()
        piece(j, source_of(j)).wait_recv()

    def parcel(p, j, source):
        to = lax.rem(leaf + offset(j), leaves)
        return send(
            send2.at[p, to], mine.at[p, source], cs.at[p, j - 1], cr.at[p, j - 1], leaf=to
        )

    def collect(p, d):
        children = [slots_ref[d * par_dev + p, k] for k in range(slot_count)]
        firsts = [lax.shift_right_logical(c, 4) * span for c in children]
        locals_ = [c & (stored - 1) for c in children]
        for t in range(2):
            for k in range(slot_count):
                row = held[pl.ds(firsts[k] + locals_[k] + t * stored, 1), :]
                at = t * slot_count + k
                send2[p, d, at // 4, at % 4 : at % 4 + 1, :] = row
        for n in range(slot_count // 2):
            pick = []
            for e in range(2):
                k = 2 * n + e
                row = held[
                    pl.ds(firsts[k] + 2 * stored + lax.shift_right_logical(locals_[k], 1), 1), :
                ]
                pick.append(jnp.where((locals_[k] & 1) == e, row, pltpu.roll(row, 64, 1)))
            at = 2 * slot_count + n
            send2[p, d, at // 4, at % 4 : at % 4 + 1, :] = jnp.where(left, pick[0], pick[1])

    for p in range(par_dev):

        @pl.loop(1, leaves)
        def _(j):
            collect(p, lax.rem(leaf + offset(j), leaves))
            parcel(p, j, leaf).start()

        collect(p, leaf)
        mine[p, leaf] = send2[p, leaf]

    for k in range(slot_count):
        row = jnp.zeros((1, 128), jnp.float32)
        for p in range(par_dev):
            parent = leaf * par_dev + p
            child = slots_ref[parent, k]
            value = jnp.sum(
                jnp.where(
                    lane == (child & (stored - 1)),
                    scale_all[lax.shift_right_logical(child, 4)], 0.0,
                ),
                axis=1, keepdims=True,
            )
            value = jnp.where(k < count_ref[parent], value, 0.0)
            row = jnp.where(lane == p, value, row)
        scale_out[k] = row

    def tell(j, source):
        to = lax.rem(own + j, panels)
        return send(
            scale_out.at[to], scale_in.at[source], ds.at[j - 1], dr.at[j - 1], panel=to
        )

    def slot(p, j, source):
        to = lax.rem(own + j, panels)
        at = pl.ds(pl.multiple_of((p * slot_count + to) * deep, 8), deep)
        return send(
            ready.at[at], land.at[p, source], es.at[p, j - 1], er.at[p, j - 1], panel=to
        )

    def from_of(j):
        return lax.rem(own + panels - j, panels)

    for j in range(1, panels):
        tell(j, own).start()
    scale_in[own] = scale_out[own]
    for p in range(par_dev):

        @pl.loop(1, leaves)
        def _(j):
            parcel(p, j, source_of(j)).wait_recv()

        @pl.loop(0, leaves)
        def _(i):
            base = p * slot_count * deep + i
            for t in range(2):
                for g in range(slot_count // 4):
                    at = base + g * 4 * deep + t * half
                    ready[pl.ds(at, 4, stride=deep), :] = mine[p, i, t * slot_count // 4 + g]
            for g in range(slot_count // 8):
                row = mine[p, i, slot_count // 2 + g]
                for e in range(2):
                    at = base + (g * 8 + e) * deep + 2 * half
                    ready[pl.ds(at, 4, stride=2 * deep), :] = row

        for j in range(1, panels):
            slot(p, j, own).start()
        land[p, own] = ready[
            pl.ds(pl.multiple_of((p * slot_count + own) * deep, 8), deep), :
        ]

    for j in range(1, panels):
        tell(j, from_of(j)).wait_recv()

    def decode(p, q):
        scale = scale_in[q][:, p : p + 1]
        for t in range(4):
            for n in range(2):
                if t < 3:
                    word = land[p, q, t * half : t * half + half, :]
                    code = word >> 16 if n == 0 else (word << 16) >> 16
                    v = code.astype(jnp.float32)
                    v = v * jnp.abs(v) * (scale * 0.5 if t == 0 else scale)
                    if t == 2:
                        q_side = (q % 2) ^ (q // 2 // (parts // 2))
                        v = jnp.where(core == q_side, v, pltpu.roll(v, 64, 1))
                        v = jnp.where(left if q_side == 0 else ~left, v, 0.0)
                    hi = v.astype(jnp.bfloat16)
                    lo = (v - hi.astype(jnp.float32)).astype(jnp.bfloat16)
                else:
                    hi = lo = jnp.zeros((half, 128), jnp.bfloat16)
                at = (q // 2 + t) % parts * 128
                row = q * row_block + n * half
                out_ref[p, row : row + half, at : at + 128] = hi
                out_ref[p, order + row : order + row + half, at : at + 128] = lo

    for p in range(par_dev):
        for j in range(1, panels):
            slot(p, j, from_of(j)).wait_recv()
        for q in range(panels):
            decode(p, q)

    @pl.loop(1, leaves)
    def _(j):
        piece(j, leaf).wait_send()
        scales(j, leaf).wait_send()
        for p in range(par_dev):
            parcel(p, j, leaf).wait_send()

    for j in range(1, panels):
        tell(j, own).wait_send()
        for p in range(par_dev):
            slot(p, j, own).wait_send()


def route(child_cost, parent_slots, child_count, leaves, panels):
    stored, row_block, order = child_cost.shape
    parents, slot_count = parent_slots.shape
    par_dev = parents // leaves
    half = row_block // 2
    rows = stored * 5 // 2
    groups = slot_count * 5 // 8
    vmem = pl.BlockSpec(memory_space=pltpu.VMEM)
    smem = pl.BlockSpec(memory_space=pltpu.SMEM)
    dma = pltpu.SemaphoreType.DMA
    word = lambda *shape: pltpu.VMEM(shape + (128,), jnp.int32)
    return pl.pallas_call(
        functools.partial(route_kernel, leaves, panels),
        out_shape=jax.ShapeDtypeStruct((par_dev, 2 * order, order), jnp.bfloat16),
        in_specs=[smem, smem, vmem],
        out_specs=vmem,
        scratch_shapes=[
            word(leaves * rows),
            word(leaves * rows),
            word(par_dev, leaves, groups, 4),
            word(par_dev, leaves, groups, 4),
            word(par_dev * slot_count * 3 * half),
            word(par_dev, panels, 3 * half),
            pltpu.VMEM((leaves, 1, 128), jnp.float32),
            pltpu.VMEM((slot_count, 1, 128), jnp.float32),
            pltpu.VMEM((panels, 1, 128), jnp.float32),
        ]
        + [dma((leaves - 1,))] * 4
        + [dma((par_dev, leaves - 1))] * 2
        + [dma((panels - 1,))] * 2
        + [dma((par_dev, panels - 1))] * 2,
        compiler_params=pltpu.CompilerParams(
            collective_id=1, has_side_effects=True, vmem_limit_bytes=40 << 20
        ),
        name="route",
    )(parent_slots, child_count, child_cost)


def per_device(child_cost, panel, section_weight, parent_slots, child_count):
    leaves = lax.axis_size("leaf")
    panels = lax.axis_size("panel")
    order = child_cost.shape[2]
    both = route(child_cost, parent_slots, child_count, leaves, panels)
    prod = jnp.einsum("prs,psz->prz", both, panel, preferred_element_type=jnp.float32)
    hi, lo = split(prod[:, :order] + prod[:, order:])
    partial_sum = jnp.einsum(
        "paz,pay->pzy",
        jnp.concatenate([panel, panel], axis=1),
        jnp.concatenate([hi, lo], axis=1),
        preferred_element_type=jnp.float32,
    )
    h1, h22 = reduce(partial_sum + jnp.swapaxes(partial_sum, 1, 2), panels)
    return finish(h1, h22, section_weight, panels)


def solution(mesh):
    in_specs = (P("leaf", "panel", None), P("leaf", "panel", None), P("leaf", None), P(), P())
    out_specs = (P("leaf", "panel", None), P("leaf", "panel", None))
    return jax.shard_map(
        per_device, mesh=mesh, in_specs=in_specs, out_specs=out_specs, check_vma=False
    )
```

```python
import functools

import jax
import jax.numpy as jnp
from jax import lax
from jax.experimental import pallas as pl
from jax.experimental.pallas import tpu as pltpu
from jax.sharding import PartitionSpec as P

NU = 128
HI = lax.Precision.HIGHEST


def pivots(cols, sub):
    for k in range(8):
        inv = 1.0 / jnp.broadcast_to(cols[k][k : k + 1, :], (8, 128))
        rows = [c[k : k + 1, :] * inv for c in cols]
        pivot = cols[k]
        cols = [
            jnp.where(sub == k, inv if j == k else rows[j], (0.0 if j == k else c) - pivot * (inv if j == k else rows[j]))
            for j, c in enumerate(cols)
        ]
    return cols


def sweep(blocks):
    lane = lax.broadcasted_iota(jnp.int32, (8, 128), 1)
    sub = lax.broadcasted_iota(jnp.int32, (8, 128), 0)

    def body(_, carry):
        out = []
        tops = []
        for mat in carry:
            top = mat[0]
            cols = [jnp.broadcast_to(top[:, j : j + 1], (8, 128)) for j in range(8)]
            cols = pivots(cols, sub)
            new = cols[0] * top[0:1, :]
            for j in range(1, 8):
                new = new + cols[j] * top[j : j + 1, :]
            for j in range(8):
                new = jnp.where(lane == j, cols[j], new)
            tops.append(new)
        for mat, top in zip(carry, tops):
            moved = []
            for blk in mat[1:]:
                new = jnp.where(lane < 8, 0.0, blk)
                for j in range(8):
                    new = new - blk[:, j : j + 1] * top[j : j + 1, :]
                moved.append(pltpu.roll(new, 120, 1))
            moved.append(pltpu.roll(top, 120, 1))
            out.append(tuple(moved))
        return tuple(out)

    return lax.fori_loop(0, 16, body, blocks)


def solve_kernel(
    panels, t_ref, a_ref, weight_ref, cost_ref, gain_ref,
    high, low, half_sum, part, h1, h2, mate1, mate2, acc1, acc2, in1, in2, inv_ref,
    m1s, m1r, m2s, m2r, d1s, d1r, d2s, d2r, gs, gr,
):
    own = lax.axis_index("panel")
    par_dev, order, _ = a_ref.shape
    chips = panels // 2
    chip, core = own // 2, own % 2
    mate = 2 * chip + 1 - core
    n1, n2 = gain_ref.shape[1], cost_ref.shape[1]
    tiles = order // 128

    def send(src, dst, ssem, rsem, to):
        return pltpu.make_async_remote_copy(
            src_ref=src, dst_ref=dst, send_sem=ssem, recv_sem=rsem,
            device_id={"panel": to}, device_id_type=pl.DeviceIdType.MESH,
        )

    barrier = pltpu.get_barrier_semaphore()
    for j in range(1, panels):
        pl.semaphore_signal(
            barrier, inc=1, device_id={"panel": lax.rem(own + j, panels)},
            device_id_type=pl.DeviceIdType.MESH,
        )

    @pl.loop(0, par_dev * tiles)
    def _(n):
        p, i = n // tiles, lax.rem(n, tiles)
        rows = pl.ds(pl.multiple_of(i * 128, 128), 128)
        low_rows = pl.ds(pl.multiple_of(order + i * 128, 128), 128)
        a = a_ref[p]
        prod = jnp.dot(t_ref[p, rows, :], a, preferred_element_type=jnp.float32)
        prod = prod + jnp.dot(t_ref[p, low_rows, :], a, preferred_element_type=jnp.float32)
        top = prod.astype(jnp.bfloat16)
        high[p, rows, :] = top
        low[p, rows, :] = (prod - top.astype(jnp.float32)).astype(jnp.bfloat16)

    @pl.loop(0, par_dev * tiles)
    def _(n):
        p, i = n // tiles, lax.rem(n, tiles)
        rows = pl.ds(pl.multiple_of(i * 128, 128), 128)
        a = a_ref[p, :, rows]
        total = [
            lax.dot_general(
                a, x[p], (((0,), (0,)), ((), ())), preferred_element_type=jnp.float32
            )
            for x in (high, low)
        ]
        half_sum[p, rows, :] = total[0] + total[1]

    def mirror(p, i):
        rows = slice(i * 128, i * 128 + 128)
        for j in range(tiles):
            cols = slice(j * 128, j * 128 + 128)
            part[p, rows, cols] = half_sum[p, rows, cols] + half_sum[p, cols, rows].T

    def rows1(t, c):
        return pl.ds(pl.multiple_of((2 * t + c) * n1, 8), n1)

    def rows2(t, c):
        return pl.ds(pl.multiple_of(NU + (2 * t + c) * n2, 8), n2)

    first = [
        send(part.at[:, rows1(t, 1 - core), :], mate1.at[t], m1s.at[t], m1r.at[t], mate)
        for t in range(chips)
    ]
    second = [
        send(part.at[:, rows2(t, 1 - core), :], mate2.at[t], m2s.at[t], m2r.at[t], mate)
        for t in range(chips)
    ]
    for p in range(par_dev):
        mirror(p, 0)
    pl.semaphore_wait(barrier, panels - 1)
    for copy in first:
        copy.start()
    for p in range(par_dev):
        for i in range(1, tiles):
            mirror(p, i)
    for copy in second:
        copy.start()
    others = [lax.rem(chip + j, chips) for j in range(1, chips)]

    def spread(acc, land, ssem, rsem):
        return [
            send(acc.at[o], land.at[j], ssem.at[j], rsem.at[j], 2 * o + core)
            for j, o in enumerate(others)
        ]

    for t in range(chips):
        first[t].wait_recv()
        acc1[t] = part[:, rows1(t, core), :] + mate1[t]
    out1 = spread(acc1, in1, d1s, d1r)
    for copy in out1:
        copy.start()
    for t in range(chips):
        second[t].wait_recv()
        acc2[t] = part[:, rows2(t, core), :] + mate2[t]
    for copy in out1:
        copy.wait_recv()
    total = acc1[chip]
    for j in range(chips - 1):
        total = total + in1[j]
    h1[own] = total
    share = [
        send(h1.at[own], h1.at[own], gs.at[j - 1], gr.at[j - 1], lax.rem(own + j, panels))
        for j in range(1, panels)
    ]
    for copy in share:
        copy.start()
    out2 = spread(acc2, in2, d2s, d2r)
    for j in range(1, panels):
        source = lax.rem(own + panels - j, panels)
        send(
            h1.at[source], h1.at[source], gs.at[j - 1], gr.at[j - 1],
            lax.rem(own + j, panels),
        ).wait_recv()
    for copy in out2:
        copy.start()

    lane = lax.broadcasted_iota(jnp.int32, (8, 128), 1)
    sub = lax.broadcasted_iota(jnp.int32, (8, 128), 0)
    mats = []
    for p in range(par_dev):
        blocks = []
        for b in range(NU // 8):
            at = b * 8
            blk = h1[at // n1, p, at % n1 : at % n1 + 8, :NU]
            blocks.append(blk + jnp.where(lane == sub + at, weight_ref[p : p + 1, :NU], 0.0))
        mats.append(tuple(blocks))
    mats = sweep(tuple(mats))
    for p in range(par_dev):
        for b in range(NU // 8):
            inv_ref[p, b * 8 : b * 8 + 8, :] = mats[p][b]
    solved = []
    for p in range(par_dev):
        cross = jnp.concatenate([h1[q, p, :, NU:] for q in range(panels)], axis=0)
        own_rows = inv_ref[p, pl.ds(pl.multiple_of(own * n1, 8), n1), :]
        solved.append(
            jnp.dot(inv_ref[p], cross, precision=HI, preferred_element_type=jnp.float32)
        )
        gain_ref[p] = -jnp.dot(own_rows, cross, precision=HI, preferred_element_type=jnp.float32)
    for copy in out2:
        copy.wait_recv()
    total = acc2[chip]
    for j in range(chips - 1):
        total = total + in2[j]
    h2[...] = total
    width = order - NU
    on_diag = lax.broadcasted_iota(jnp.int32, (n2, width), 1) == (
        lax.broadcasted_iota(jnp.int32, (n2, width), 0) + own * n2
    )
    for p in range(par_dev):
        cost_ref[p] = (
            h2[p, :, NU:]
            + jnp.where(on_diag, weight_ref[p : p + 1, NU:], 0.0)
            - jnp.dot(h2[p, :, :NU], solved[p], precision=HI, preferred_element_type=jnp.float32)
        )
    for copy in first + second + out1 + out2 + share:
        copy.wait_send()


def solve(coded, panel, section_weight, panels):
    par_dev, order, _ = panel.shape
    chips = panels // 2
    n1, n2 = NU // panels, (order - NU) // panels
    one = (par_dev, n1, order)
    two = (par_dev, n2, order)
    vmem = pl.BlockSpec(memory_space=pltpu.VMEM)
    dma = pltpu.SemaphoreType.DMA
    f32 = lambda *shape: pltpu.VMEM(shape, jnp.float32)
    return pl.pallas_call(
        functools.partial(solve_kernel, panels),
        out_shape=(
            jax.ShapeDtypeStruct((par_dev, n2, order - NU), jnp.float32),
            jax.ShapeDtypeStruct((par_dev, n1, order - NU), jnp.float32),
        ),
        in_specs=[vmem] * 3,
        out_specs=(vmem, vmem),
        scratch_shapes=[
            pltpu.VMEM((par_dev, order, order), jnp.bfloat16),
            pltpu.VMEM((par_dev, order, order), jnp.bfloat16),
            f32(par_dev, order, order),
            f32(par_dev, order, order),
            f32(panels, *one),
            f32(*two),
            f32(chips, *one),
            f32(chips, *two),
            f32(chips, *one),
            f32(chips, *two),
            f32(chips - 1, *one),
            f32(chips - 1, *two),
            f32(par_dev, NU, NU),
        ]
        + [dma((chips,))] * 4
        + [dma((chips - 1,))] * 4
        + [dma((panels - 1,))] * 2,
        compiler_params=pltpu.CompilerParams(
            collective_id=0, has_side_effects=True, vmem_limit_bytes=40 << 20
        ),
        name="solve",
    )(coded, panel, section_weight)


CODE = 32767.0


def route_kernel(
    leaves, panels, slots_ref, count_ref, child_ref, out_ref,
    send1, held, send2, mine, ready, land, scale_all, scale_out, scale_in,
    as_, ar, bs, br, cs, cr, ds, dr, es, er,
):
    leaf = lax.axis_index("leaf")
    own = lax.axis_index("panel")
    stored, row_block, order = child_ref.shape
    par_dev, _, groups = send2.shape[:3]
    slot_count = slots_ref.shape[1]
    half = row_block // 2
    parts = order // 128
    lane = lax.broadcasted_iota(jnp.int32, (1, 128), 1)
    left = lane < 64
    span = held.shape[0] // leaves
    deep = 3 * half

    def offset(j):
        step = (j + 1) // 2
        return step + (leaves - 2 * step) * (1 - lax.rem(j, 2))

    def send(src, dst, ssem, rsem, **to):
        return pltpu.make_async_remote_copy(
            src_ref=src, dst_ref=dst, send_sem=ssem, recv_sem=rsem,
            device_id=to, device_id_type=pl.DeviceIdType.MESH,
        )

    barrier = pltpu.get_barrier_semaphore()

    @pl.loop(1, leaves)
    def _(j):
        pl.semaphore_signal(
            barrier, inc=1, device_id={"leaf": lax.rem(leaf + j, leaves)},
            device_id_type=pl.DeviceIdType.MESH,
        )

    for j in range(1, panels):
        pl.semaphore_signal(
            barrier, inc=1, device_id={"panel": lax.rem(own + j, panels)},
            device_id_type=pl.DeviceIdType.MESH,
        )

    chip, core = own // 2, own % 2
    upper = chip // (parts // 2)
    side = core + upper - 2 * core * upper

    def encode(c, row):
        cols = [pl.ds(pl.multiple_of(lax.rem(chip + t, parts) * 128, 128), 128) for t in range(3)]
        blocks = [child_ref[c, :, at] for at in cols]
        tops = [jnp.max(jnp.abs(x), keepdims=True) for x in blocks]
        top = jnp.maximum(jnp.maximum(tops[0], tops[1]), jnp.maximum(tops[2], 1e-30))
        inv = 1.0 / top
        words = []
        for x in blocks:
            x = x * inv
            size = (jnp.sqrt(jnp.abs(x)) * CODE + 0.5).astype(jnp.int32)
            code = jnp.where(x < 0, -size, size)
            words.append(code[:half] * 65536 + (code[half:] & 65535))
        for t in range(2):
            send1[pl.ds(t * stored + c, half, stride=span), :] = words[t]
        return words[2], jnp.where(lane == c, top * (1.0 / (CODE * CODE)), row)

    def encode_pair(n, row):
        even, row = encode(2 * n, row)
        odd, row = encode(2 * n + 1, row)
        even = jnp.where(side == 0, even, pltpu.roll(even, 64, 1))
        odd = jnp.where(side == 1, odd, pltpu.roll(odd, 64, 1))
        send1[pl.ds(2 * stored + n, half, stride=span), :] = jnp.where(left, even, odd)
        return row

    scale_all[leaf] = lax.fori_loop(
        0, stored // 2, encode_pair, jnp.zeros((1, 128), jnp.float32)
    )
    pl.semaphore_wait(barrier, leaves + panels - 2)

    def message(i):
        return pl.ds(pl.multiple_of(i * span, 8), span)

    def piece(j, source):
        to = lax.rem(leaf + offset(j), leaves)
        return send(
            send1.at[message(to)], held.at[message(source)],
            as_.at[j - 1], ar.at[j - 1], leaf=to,
        )

    def scales(j, source):
        return send(
            scale_all.at[leaf], scale_all.at[source], bs.at[j - 1], br.at[j - 1],
            leaf=lax.rem(leaf + offset(j), leaves),
        )

    def source_of(j):
        return lax.rem(leaf + leaves - offset(j), leaves)

    @pl.loop(1, leaves)
    def _(j):
        piece(j, leaf).start()
        scales(j, leaf).start()

    held[message(leaf), :] = send1[message(leaf), :]

    @pl.loop(1, leaves)
    def _(j):
        scales(j, source_of(j)).wait_recv()
        piece(j, source_of(j)).wait_recv()

    def parcel(p, j, source):
        to = lax.rem(leaf + offset(j), leaves)
        return send(
            send2.at[p, to], mine.at[p, source], cs.at[p, j - 1], cr.at[p, j - 1], leaf=to
        )

    def collect(p, d):
        children = [slots_ref[d * par_dev + p, k] for k in range(slot_count)]
        firsts = [lax.shift_right_logical(c, 4) * span for c in children]
        locals_ = [c & (stored - 1) for c in children]
        for t in range(2):
            for k in range(slot_count):
                row = held[pl.ds(firsts[k] + locals_[k] + t * stored, 1), :]
                at = t * slot_count + k
                send2[p, d, at // 4, at % 4 : at % 4 + 1, :] = row
        for n in range(slot_count // 2):
            pick = []
            for e in range(2):
                k = 2 * n + e
                row = held[
                    pl.ds(firsts[k] + 2 * stored + lax.shift_right_logical(locals_[k], 1), 1), :
                ]
                pick.append(jnp.where((locals_[k] & 1) == e, row, pltpu.roll(row, 64, 1)))
            at = 2 * slot_count + n
            send2[p, d, at // 4, at % 4 : at % 4 + 1, :] = jnp.where(left, pick[0], pick[1])

    for p in range(par_dev):

        @pl.loop(1, leaves)
        def _(j):
            collect(p, lax.rem(leaf + offset(j), leaves))
            parcel(p, j, leaf).start()

        collect(p, leaf)
        mine[p, leaf] = send2[p, leaf]

    for k in range(slot_count):
        row = jnp.zeros((1, 128), jnp.float32)
        for p in range(par_dev):
            parent = leaf * par_dev + p
            child = slots_ref[parent, k]
            value = jnp.sum(
                jnp.where(
                    lane == (child & (stored - 1)),
                    scale_all[lax.shift_right_logical(child, 4)], 0.0,
                ),
                axis=1, keepdims=True,
            )
            value = jnp.where(k < count_ref[parent], value, 0.0)
            row = jnp.where(lane == p, value, row)
        scale_out[k] = row

    def tell(j, source):
        to = lax.rem(own + j, panels)
        return send(
            scale_out.at[to], scale_in.at[source], ds.at[j - 1], dr.at[j - 1], panel=to
        )

    def slot(p, j, source):
        to = lax.rem(own + j, panels)
        at = pl.ds(pl.multiple_of((p * slot_count + to) * deep, 8), deep)
        return send(
            ready.at[at], land.at[p, source], es.at[p, j - 1], er.at[p, j - 1], panel=to
        )

    def from_of(j):
        return lax.rem(own + panels - j, panels)

    for j in range(1, panels):
        tell(j, own).start()
    scale_in[own] = scale_out[own]
    for p in range(par_dev):

        @pl.loop(1, leaves)
        def _(j):
            parcel(p, j, source_of(j)).wait_recv()

        @pl.loop(0, leaves)
        def _(i):
            base = p * slot_count * deep + i
            for t in range(2):
                for g in range(slot_count // 4):
                    at = base + g * 4 * deep + t * half
                    ready[pl.ds(at, 4, stride=deep), :] = mine[p, i, t * slot_count // 4 + g]
            for g in range(slot_count // 8):
                row = mine[p, i, slot_count // 2 + g]
                for e in range(2):
                    at = base + (g * 8 + e) * deep + 2 * half
                    ready[pl.ds(at, 4, stride=2 * deep), :] = row

        for j in range(1, panels):
            slot(p, j, own).start()
        land[p, own] = ready[
            pl.ds(pl.multiple_of((p * slot_count + own) * deep, 8), deep), :
        ]

    for j in range(1, panels):
        tell(j, from_of(j)).wait_recv()

    def decode(p, q):
        scale = scale_in[q][:, p : p + 1]
        for t in range(4):
            for n in range(2):
                if t < 3:
                    word = land[p, q, t * half : t * half + half, :]
                    code = word >> 16 if n == 0 else (word << 16) >> 16
                    v = code.astype(jnp.float32)
                    v = v * jnp.abs(v) * (scale * 0.5 if t == 0 else scale)
                    if t == 2:
                        q_side = (q % 2) ^ (q // 2 // (parts // 2))
                        v = jnp.where(core == q_side, v, pltpu.roll(v, 64, 1))
                        v = jnp.where(left if q_side == 0 else ~left, v, 0.0)
                    hi = v.astype(jnp.bfloat16)
                    lo = (v - hi.astype(jnp.float32)).astype(jnp.bfloat16)
                else:
                    hi = lo = jnp.zeros((half, 128), jnp.bfloat16)
                at = (q // 2 + t) % parts * 128
                row = q * row_block + n * half
                out_ref[p, row : row + half, at : at + 128] = hi
                out_ref[p, order + row : order + row + half, at : at + 128] = lo

    for p in range(par_dev):
        for j in range(1, panels):
            slot(p, j, from_of(j)).wait_recv()
        for q in range(panels):
            decode(p, q)

    @pl.loop(1, leaves)
    def _(j):
        piece(j, leaf).wait_send()
        scales(j, leaf).wait_send()
        for p in range(par_dev):
            parcel(p, j, leaf).wait_send()

    for j in range(1, panels):
        tell(j, own).wait_send()
        for p in range(par_dev):
            slot(p, j, own).wait_send()


def route(child_cost, parent_slots, child_count, leaves, panels):
    stored, row_block, order = child_cost.shape
    parents, slot_count = parent_slots.shape
    par_dev = parents // leaves
    half = row_block // 2
    rows = stored * 5 // 2
    groups = slot_count * 5 // 8
    vmem = pl.BlockSpec(memory_space=pltpu.VMEM)
    smem = pl.BlockSpec(memory_space=pltpu.SMEM)
    dma = pltpu.SemaphoreType.DMA
    word = lambda *shape: pltpu.VMEM(shape + (128,), jnp.int32)
    return pl.pallas_call(
        functools.partial(route_kernel, leaves, panels),
        out_shape=jax.ShapeDtypeStruct((par_dev, 2 * order, order), jnp.bfloat16),
        in_specs=[smem, smem, vmem],
        out_specs=vmem,
        scratch_shapes=[
            word(leaves * rows),
            word(leaves * rows),
            word(par_dev, leaves, groups, 4),
            word(par_dev, leaves, groups, 4),
            word(par_dev * slot_count * 3 * half),
            word(par_dev, panels, 3 * half),
            pltpu.VMEM((leaves, 1, 128), jnp.float32),
            pltpu.VMEM((slot_count, 1, 128), jnp.float32),
            pltpu.VMEM((panels, 1, 128), jnp.float32),
        ]
        + [dma((leaves - 1,))] * 4
        + [dma((par_dev, leaves - 1))] * 2
        + [dma((panels - 1,))] * 2
        + [dma((par_dev, panels - 1))] * 2,
        compiler_params=pltpu.CompilerParams(
            collective_id=1, has_side_effects=True, vmem_limit_bytes=40 << 20
        ),
        name="route",
    )(parent_slots, child_count, child_cost)


def per_device(child_cost, panel, section_weight, parent_slots, child_count):
    leaves = lax.axis_size("leaf")
    panels = lax.axis_size("panel")
    coded = route(child_cost, parent_slots, child_count, leaves, panels)
    return solve(coded, panel, section_weight, panels)


def solution(mesh):
    in_specs = (P("leaf", "panel", None), P("leaf", "panel", None), P("leaf", None), P(), P())
    out_specs = (P("leaf", "panel", None), P("leaf", "panel", None))
    return jax.shard_map(
        per_device, mesh=mesh, in_specs=in_specs, out_specs=out_specs, check_vma=False
    )
```

```python
import functools

import jax
import jax.numpy as jnp
from jax import lax
from jax.experimental import pallas as pl
from jax.experimental.pallas import tpu as pltpu
from jax.sharding import PartitionSpec as P

NU = 128
HI = lax.Precision.HIGHEST


def pivots(cols, sub):
    for k in range(8):
        inv = 1.0 / jnp.broadcast_to(cols[k][k : k + 1, :], (8, 128))
        rows = [inv if j == k else c[k : k + 1, :] * inv for j, c in enumerate(cols)]
        pivot = cols[k]
        cols = [
            jnp.where(sub == k, rows[j], (0.0 if j == k else c) - pivot * rows[j])
            for j, c in enumerate(cols)
        ]
    return cols


def eight(top, other, at, lane, sub):
    cols = [jnp.broadcast_to(top[:, at + j : at + j + 1], (8, 128)) for j in range(8)]
    cols = pivots(cols, sub)
    new = cols[0] * top[0:1, :]
    for j in range(1, 8):
        new = new + cols[j] * top[j : j + 1, :]
    for j in range(8):
        new = jnp.where(lane == at + j, cols[j], new)
    rest = jnp.where((lane >= at) & (lane < at + 8), 0.0, other)
    for j in range(8):
        rest = rest - other[:, at + j : at + j + 1] * new[j : j + 1, :]
    return new, rest


def sweep(mats, start, stop):
    lane = lax.broadcasted_iota(jnp.int32, (8, 128), 1)
    sub = lax.broadcasted_iota(jnp.int32, (8, 128), 0)
    wide = lax.broadcasted_iota(jnp.int32, (NU - 16, 128), 1)

    def body(_, carry):
        out = []
        for mat in carry:
            one, two = eight(mat[:8], mat[8:16], 0, lane, sub)
            two, one = eight(two, one, 8, lane, sub)
            top = jnp.concatenate([one, two], axis=0)
            rest = mat[16:]
            new = jnp.where(wide < 16, 0.0, rest) - jnp.dot(
                rest[:, :16], top, precision=HI, preferred_element_type=jnp.float32
            )
            out.append(pltpu.roll(jnp.concatenate([new, top], axis=0), 112, 1))
        return tuple(out)

    return lax.fori_loop(start, stop, body, mats)


def solve_kernel(
    panels, t_ref, a_ref, weight_ref, cost_ref, gain_ref,
    high, low, half_sum, part, mate1, mate2, h0, h1, acc0, acc1, acc2, in0, in1, in2, inv_ref,
    m1s, m1r, m2s, m2r, d0s, d0r, d1s, d1r, d2s, d2r, g0s, g0r, g1s, g1r,
):
    own = lax.axis_index("panel")
    par_dev, order, _ = a_ref.shape
    chips = panels // 2
    chip, core = own // 2, own % 2
    mate = 2 * chip + 1 - core
    n1, n2 = gain_ref.shape[1], cost_ref.shape[1]
    tiles = order // 128

    def send(src, dst, ssem, rsem, to):
        return pltpu.make_async_remote_copy(
            src_ref=src, dst_ref=dst, send_sem=ssem, recv_sem=rsem,
            device_id={"panel": to}, device_id_type=pl.DeviceIdType.MESH,
        )

    barrier = pltpu.get_barrier_semaphore()
    for j in range(1, panels):
        pl.semaphore_signal(
            barrier, inc=1, device_id={"panel": lax.rem(own + j, panels)},
            device_id_type=pl.DeviceIdType.MESH,
        )

    @pl.loop(0, par_dev * tiles)
    def _(n):
        p, i = n // tiles, lax.rem(n, tiles)
        rows = pl.ds(pl.multiple_of(i * 128, 128), 128)
        low_rows = pl.ds(pl.multiple_of(order + i * 128, 128), 128)
        a = a_ref[p]
        prod = jnp.dot(t_ref[p, rows, :], a, preferred_element_type=jnp.float32)
        prod = prod + jnp.dot(t_ref[p, low_rows, :], a, preferred_element_type=jnp.float32)
        top = prod.astype(jnp.bfloat16)
        high[p, rows, :] = top
        low[p, rows, :] = (prod - top.astype(jnp.float32)).astype(jnp.bfloat16)

    @pl.loop(0, par_dev * tiles)
    def _(n):
        p, i = n // tiles, lax.rem(n, tiles)
        rows = pl.ds(pl.multiple_of(i * 128, 128), 128)
        a = a_ref[p, :, rows]
        total = [
            lax.dot_general(
                a, x[p], (((0,), (0,)), ((), ())), preferred_element_type=jnp.float32
            )
            for x in (high, low)
        ]
        half_sum[p, rows, :] = total[0] + total[1]

    def mirror(p, i):
        rows = slice(i * 128, i * 128 + 128)
        for j in range(tiles):
            cols = slice(j * 128, j * 128 + 128)
            part[p, rows, cols] = half_sum[p, rows, cols] + half_sum[p, cols, rows].T

    def rows1(t, c):
        return pl.ds(pl.multiple_of((2 * t + c) * n1, 8), n1)

    def rows2(t, c):
        return pl.ds(pl.multiple_of(NU + (2 * t + c) * n2, 8), n2)

    first = [
        send(part.at[:, rows1(t, 1 - core), :], mate1.at[t], m1s.at[t], m1r.at[t], mate)
        for t in range(chips)
    ]
    second = [
        send(part.at[:, rows2(t, 1 - core), NU:], mate2.at[t], m2s.at[t], m2r.at[t], mate)
        for t in range(chips)
    ]
    for p in range(par_dev):
        mirror(p, 0)
    pl.semaphore_wait(barrier, panels - 1)
    for copy in first:
        copy.start()
    for p in range(par_dev):
        for i in range(1, tiles):
            mirror(p, i)
    for copy in second:
        copy.start()
    others = [lax.rem(chip + j, chips) for j in range(1, chips)]

    def spread(acc, land, ssem, rsem):
        return [
            send(acc.at[o], land.at[j], ssem.at[j], rsem.at[j], 2 * o + core)
            for j, o in enumerate(others)
        ]

    def gathered(ref, ssem, rsem, source):
        return [
            send(ref.at[at], ref.at[at], ssem.at[j - 1], rsem.at[j - 1], lax.rem(own + j, panels))
            for j, at in ((j, source(j)) for j in range(1, panels))
        ]

    def summed(acc, land):
        total = acc[chip]
        for j in range(chips - 1):
            total = total + land[j]
        return total

    for t in range(chips):
        first[t].wait_recv()
        acc0[t] = part[:, rows1(t, core), :NU] + mate1[t, :, :, :NU]
    out0 = spread(acc0, in0, d0s, d0r)
    for copy in out0:
        copy.start()
    for t in range(chips):
        acc1[t] = part[:, rows1(t, core), NU:] + mate1[t, :, :, NU:]
    out1 = spread(acc1, in1, d1s, d1r)
    for copy in out1:
        copy.start()
    for copy in out0:
        copy.wait_recv()
    h0[own] = summed(acc0, in0)
    share0 = gathered(h0, g0s, g0r, lambda j: own)
    for copy in share0:
        copy.start()
    for t in range(chips):
        second[t].wait_recv()
        acc2[t] = part[:, rows2(t, core), NU:] + mate2[t]
    for copy in out1:
        copy.wait_recv()
    h1[own] = summed(acc1, in1)
    share1 = gathered(h1, g1s, g1r, lambda j: own)
    for copy in share1:
        copy.start()
    out2 = spread(acc2, in2, d2s, d2r)
    for copy in out2:
        copy.start()
    for copy in gathered(h0, g0s, g0r, lambda j: lax.rem(own + panels - j, panels)):
        copy.wait_recv()

    row = lax.broadcasted_iota(jnp.int32, (NU, NU), 0)
    col = lax.broadcasted_iota(jnp.int32, (NU, NU), 1)
    mats = []
    for p in range(par_dev):
        mat = jnp.concatenate([h0[q, p] for q in range(panels)], axis=0)
        mats.append(mat + jnp.where(row == col, weight_ref[p : p + 1, :NU], 0.0))
    mats = sweep(tuple(mats), 0, NU // 16)
    for p in range(par_dev):
        inv_ref[p] = mats[p]
    for copy in gathered(h1, g1s, g1r, lambda j: lax.rem(own + panels - j, panels)):
        copy.wait_recv()
    width = order - NU
    on_diag = lax.broadcasted_iota(jnp.int32, (n2, width), 1) == (
        lax.broadcasted_iota(jnp.int32, (n2, width), 0) + own * n2
    )
    pick = jnp.where(on_diag, 1.0, 0.0)
    product = functools.partial(
        lax.dot_general, precision=HI, preferred_element_type=jnp.float32
    )
    taken = []
    for p in range(par_dev):
        cross = jnp.concatenate([h1[q, p] for q in range(panels)], axis=0)
        own_rows = inv_ref[p, pl.ds(pl.multiple_of(own * n1, 8), n1), :]
        gain_ref[p] = -product(own_rows, cross, (((1,), (0,)), ((), ())))
        own_cross = product(pick, cross, (((1,), (1,)), ((), ())))
        left = product(own_cross, inv_ref[p], (((1,), (0,)), ((), ())))
        taken.append(product(left, cross, (((1,), (0,)), ((), ()))))
    for copy in out2:
        copy.wait_recv()
    for p in range(par_dev):
        total = acc2[chip, p]
        for j in range(chips - 1):
            total = total + in2[j, p]
        cost_ref[p] = (
            total + jnp.where(on_diag, weight_ref[p : p + 1, NU:], 0.0) - taken[p]
        )
    for copy in first + second + out0 + out1 + out2 + share0 + share1:
        copy.wait_send()


def solve(coded, panel, section_weight, panels):
    par_dev, order, _ = panel.shape
    chips = panels // 2
    n1, n2 = NU // panels, (order - NU) // panels
    zero, one, two = (par_dev, n1, NU), (par_dev, n1, order - NU), (par_dev, n2, order - NU)
    vmem = pl.BlockSpec(memory_space=pltpu.VMEM)
    dma = pltpu.SemaphoreType.DMA
    f32 = lambda *shape: pltpu.VMEM(shape, jnp.float32)
    return pl.pallas_call(
        functools.partial(solve_kernel, panels),
        out_shape=(
            jax.ShapeDtypeStruct((par_dev, n2, order - NU), jnp.float32),
            jax.ShapeDtypeStruct((par_dev, n1, order - NU), jnp.float32),
        ),
        in_specs=[vmem] * 3,
        out_specs=(vmem, vmem),
        scratch_shapes=[
            pltpu.VMEM((par_dev, order, order), jnp.bfloat16),
            pltpu.VMEM((par_dev, order, order), jnp.bfloat16),
            f32(par_dev, order, order),
            f32(par_dev, order, order),
            f32(chips, par_dev, n1, order),
            f32(chips, *two),
            f32(panels, *zero),
            f32(panels, *one),
            f32(chips, *zero),
            f32(chips, *one),
            f32(chips, *two),
            f32(chips - 1, *zero),
            f32(chips - 1, *one),
            f32(chips - 1, *two),
            f32(par_dev, NU, NU),
        ]
        + [dma((chips,))] * 4
        + [dma((chips - 1,))] * 6
        + [dma((panels - 1,))] * 4,
        compiler_params=pltpu.CompilerParams(
            collective_id=0, has_side_effects=True, vmem_limit_bytes=40 << 20
        ),
        name="solve",
    )(coded, panel, section_weight)


CODE = 32767.0


def route_kernel(
    leaves, panels, slots_ref, count_ref, child_ref, out_ref,
    send1, held, send2, mine, ready, land, scale_all, scale_out, scale_in,
    as_, ar, bs, br, cs, cr, ds, dr, es, er,
):
    leaf = lax.axis_index("leaf")
    own = lax.axis_index("panel")
    stored, row_block, order = child_ref.shape
    par_dev, _, groups = send2.shape[:3]
    slot_count = slots_ref.shape[1]
    half = row_block // 2
    parts = order // 128
    lane = lax.broadcasted_iota(jnp.int32, (1, 128), 1)
    left = lane < 64
    span = held.shape[0] // leaves
    deep = 3 * half

    def offset(j):
        step = (j + 1) // 2
        return step + (leaves - 2 * step) * (1 - lax.rem(j, 2))

    def send(src, dst, ssem, rsem, **to):
        return pltpu.make_async_remote_copy(
            src_ref=src, dst_ref=dst, send_sem=ssem, recv_sem=rsem,
            device_id=to, device_id_type=pl.DeviceIdType.MESH,
        )

    barrier = pltpu.get_barrier_semaphore()

    @pl.loop(1, leaves)
    def _(j):
        pl.semaphore_signal(
            barrier, inc=1, device_id={"leaf": lax.rem(leaf + j, leaves)},
            device_id_type=pl.DeviceIdType.MESH,
        )

    for j in range(1, panels):
        pl.semaphore_signal(
            barrier, inc=1, device_id={"panel": lax.rem(own + j, panels)},
            device_id_type=pl.DeviceIdType.MESH,
        )

    chip, core = own // 2, own % 2
    upper = chip // (parts // 2)
    side = core + upper - 2 * core * upper

    def encode(c, row):
        cols = [pl.ds(pl.multiple_of(lax.rem(chip + t, parts) * 128, 128), 128) for t in range(3)]
        blocks = [child_ref[c, :, at] for at in cols]
        tops = [jnp.max(jnp.abs(x), keepdims=True) for x in blocks]
        top = jnp.maximum(jnp.maximum(tops[0], tops[1]), jnp.maximum(tops[2], 1e-30))
        inv = 1.0 / top
        words = []
        for x in blocks:
            x = x * inv
            size = (jnp.sqrt(jnp.abs(x)) * CODE + 0.5).astype(jnp.int32)
            code = jnp.where(x < 0, -size, size)
            words.append(code[:half] * 65536 + (code[half:] & 65535))
        for t in range(2):
            send1[pl.ds(t * stored + c, half, stride=span), :] = words[t]
        return words[2], jnp.where(lane == c, top * (1.0 / (CODE * CODE)), row)

    def encode_pair(n, row):
        even, row = encode(2 * n, row)
        odd, row = encode(2 * n + 1, row)
        even = jnp.where(side == 0, even, pltpu.roll(even, 64, 1))
        odd = jnp.where(side == 1, odd, pltpu.roll(odd, 64, 1))
        send1[pl.ds(2 * stored + n, half, stride=span), :] = jnp.where(left, even, odd)
        return row

    scale_all[leaf] = lax.fori_loop(
        0, stored // 2, encode_pair, jnp.zeros((1, 128), jnp.float32)
    )
    pl.semaphore_wait(barrier, leaves + panels - 2)

    def message(i):
        return pl.ds(pl.multiple_of(i * span, 8), span)

    def piece(j, source):
        to = lax.rem(leaf + offset(j), leaves)
        return send(
            send1.at[message(to)], held.at[message(source)],
            as_.at[j - 1], ar.at[j - 1], leaf=to,
        )

    def scales(j, source):
        return send(
            scale_all.at[leaf], scale_all.at[source], bs.at[j - 1], br.at[j - 1],
            leaf=lax.rem(leaf + offset(j), leaves),
        )

    def source_of(j):
        return lax.rem(leaf + leaves - offset(j), leaves)

    @pl.loop(1, leaves)
    def _(j):
        piece(j, leaf).start()
        scales(j, leaf).start()

    held[message(leaf), :] = send1[message(leaf), :]

    @pl.loop(1, leaves)
    def _(j):
        scales(j, source_of(j)).wait_recv()
        piece(j, source_of(j)).wait_recv()

    def parcel(p, j, source):
        to = lax.rem(leaf + offset(j), leaves)
        return send(
            send2.at[p, to], mine.at[p, source], cs.at[p, j - 1], cr.at[p, j - 1], leaf=to
        )

    def collect(p, d):
        children = [slots_ref[d * par_dev + p, k] for k in range(slot_count)]
        firsts = [lax.shift_right_logical(c, 4) * span for c in children]
        locals_ = [c & (stored - 1) for c in children]
        for t in range(2):
            for k in range(slot_count):
                row = held[pl.ds(firsts[k] + locals_[k] + t * stored, 1), :]
                at = t * slot_count + k
                send2[p, d, at // 4, at % 4 : at % 4 + 1, :] = row
        for n in range(slot_count // 2):
            pick = []
            for e in range(2):
                k = 2 * n + e
                row = held[
                    pl.ds(firsts[k] + 2 * stored + lax.shift_right_logical(locals_[k], 1), 1), :
                ]
                pick.append(jnp.where((locals_[k] & 1) == e, row, pltpu.roll(row, 64, 1)))
            at = 2 * slot_count + n
            send2[p, d, at // 4, at % 4 : at % 4 + 1, :] = jnp.where(left, pick[0], pick[1])

    for p in range(par_dev):

        @pl.loop(1, leaves)
        def _(j):
            collect(p, lax.rem(leaf + offset(j), leaves))
            parcel(p, j, leaf).start()

        collect(p, leaf)
        mine[p, leaf] = send2[p, leaf]

    for k in range(slot_count):
        row = jnp.zeros((1, 128), jnp.float32)
        for p in range(par_dev):
            parent = leaf * par_dev + p
            child = slots_ref[parent, k]
            value = jnp.sum(
                jnp.where(
                    lane == (child & (stored - 1)),
                    scale_all[lax.shift_right_logical(child, 4)], 0.0,
                ),
                axis=1, keepdims=True,
            )
            value = jnp.where(k < count_ref[parent], value, 0.0)
            row = jnp.where(lane == p, value, row)
        scale_out[k] = row

    def tell(j, source):
        to = lax.rem(own + j, panels)
        return send(
            scale_out.at[to], scale_in.at[source], ds.at[j - 1], dr.at[j - 1], panel=to
        )

    def slot(p, j, source):
        to = lax.rem(own + j, panels)
        at = pl.ds(pl.multiple_of((p * slot_count + to) * deep, 8), deep)
        return send(
            ready.at[at], land.at[p, source], es.at[p, j - 1], er.at[p, j - 1], panel=to
        )

    def from_of(j):
        return lax.rem(own + panels - j, panels)

    for j in range(1, panels):
        tell(j, own).start()
    scale_in[own] = scale_out[own]
    for p in range(par_dev):

        @pl.loop(1, leaves)
        def _(j):
            parcel(p, j, source_of(j)).wait_recv()

        @pl.loop(0, leaves)
        def _(i):
            base = p * slot_count * deep + i
            for t in range(2):
                for g in range(slot_count // 4):
                    at = base + g * 4 * deep + t * half
                    ready[pl.ds(at, 4, stride=deep), :] = mine[p, i, t * slot_count // 4 + g]
            for g in range(slot_count // 8):
                row = mine[p, i, slot_count // 2 + g]
                for e in range(2):
                    at = base + (g * 8 + e) * deep + 2 * half
                    ready[pl.ds(at, 4, stride=2 * deep), :] = row

        for j in range(1, panels):
            slot(p, j, own).start()
        land[p, own] = ready[
            pl.ds(pl.multiple_of((p * slot_count + own) * deep, 8), deep), :
        ]

    for j in range(1, panels):
        tell(j, from_of(j)).wait_recv()

    def decode(p, q):
        scale = scale_in[q][:, p : p + 1]
        for t in range(4):
            for n in range(2):
                if t < 3:
                    word = land[p, q, t * half : t * half + half, :]
                    code = word >> 16 if n == 0 else (word << 16) >> 16
                    v = code.astype(jnp.float32)
                    v = v * jnp.abs(v) * (scale * 0.5 if t == 0 else scale)
                    if t == 2:
                        q_side = (q % 2) ^ (q // 2 // (parts // 2))
                        v = jnp.where(core == q_side, v, pltpu.roll(v, 64, 1))
                        v = jnp.where(left if q_side == 0 else ~left, v, 0.0)
                    hi = v.astype(jnp.bfloat16)
                    lo = (v - hi.astype(jnp.float32)).astype(jnp.bfloat16)
                else:
                    hi = lo = jnp.zeros((half, 128), jnp.bfloat16)
                at = (q // 2 + t) % parts * 128
                row = q * row_block + n * half
                out_ref[p, row : row + half, at : at + 128] = hi
                out_ref[p, order + row : order + row + half, at : at + 128] = lo

    for p in range(par_dev):
        for j in range(1, panels):
            slot(p, j, from_of(j)).wait_recv()
        for q in range(panels):
            decode(p, q)

    @pl.loop(1, leaves)
    def _(j):
        piece(j, leaf).wait_send()
        scales(j, leaf).wait_send()
        for p in range(par_dev):
            parcel(p, j, leaf).wait_send()

    for j in range(1, panels):
        tell(j, own).wait_send()
        for p in range(par_dev):
            slot(p, j, own).wait_send()


def route(child_cost, parent_slots, child_count, leaves, panels):
    stored, row_block, order = child_cost.shape
    parents, slot_count = parent_slots.shape
    par_dev = parents // leaves
    half = row_block // 2
    rows = stored * 5 // 2
    groups = slot_count * 5 // 8
    vmem = pl.BlockSpec(memory_space=pltpu.VMEM)
    smem = pl.BlockSpec(memory_space=pltpu.SMEM)
    dma = pltpu.SemaphoreType.DMA
    word = lambda *shape: pltpu.VMEM(shape + (128,), jnp.int32)
    return pl.pallas_call(
        functools.partial(route_kernel, leaves, panels),
        out_shape=jax.ShapeDtypeStruct((par_dev, 2 * order, order), jnp.bfloat16),
        in_specs=[smem, smem, vmem],
        out_specs=vmem,
        scratch_shapes=[
            word(leaves * rows),
            word(leaves * rows),
            word(par_dev, leaves, groups, 4),
            word(par_dev, leaves, groups, 4),
            word(par_dev * slot_count * 3 * half),
            word(par_dev, panels, 3 * half),
            pltpu.VMEM((leaves, 1, 128), jnp.float32),
            pltpu.VMEM((slot_count, 1, 128), jnp.float32),
            pltpu.VMEM((panels, 1, 128), jnp.float32),
        ]
        + [dma((leaves - 1,))] * 4
        + [dma((par_dev, leaves - 1))] * 2
        + [dma((panels - 1,))] * 2
        + [dma((par_dev, panels - 1))] * 2,
        compiler_params=pltpu.CompilerParams(
            collective_id=1, has_side_effects=True, vmem_limit_bytes=40 << 20
        ),
        name="route",
    )(parent_slots, child_count, child_cost)


def per_device(child_cost, panel, section_weight, parent_slots, child_count):
    leaves = lax.axis_size("leaf")
    panels = lax.axis_size("panel")
    coded = route(child_cost, parent_slots, child_count, leaves, panels)
    return solve(coded, panel, section_weight, panels)


def solution(mesh):
    in_specs = (P("leaf", "panel", None), P("leaf", "panel", None), P("leaf", None), P(), P())
    out_specs = (P("leaf", "panel", None), P("leaf", "panel", None))
    return jax.shard_map(
        per_device, mesh=mesh, in_specs=in_specs, out_specs=out_specs, check_vma=False
    )
```

```python
import functools

import jax
import jax.numpy as jnp
from jax import lax
from jax.experimental import pallas as pl
from jax.experimental.pallas import tpu as pltpu
from jax.sharding import PartitionSpec as P

NU = 128
HI = lax.Precision.HIGHEST


def pivots(cols, sub):
    for k in range(8):
        inv = 1.0 / jnp.broadcast_to(cols[k][k : k + 1, :], (8, 128))
        rows = [inv if j == k else c[k : k + 1, :] * inv for j, c in enumerate(cols)]
        pivot = cols[k]
        cols = [
            jnp.where(sub == k, rows[j], (0.0 if j == k else c) - pivot * rows[j])
            for j, c in enumerate(cols)
        ]
    return cols


def eight(top, other, at, lane, sub):
    cols = [jnp.broadcast_to(top[:, at + j : at + j + 1], (8, 128)) for j in range(8)]
    cols = pivots(cols, sub)
    new = cols[0] * top[0:1, :]
    for j in range(1, 8):
        new = new + cols[j] * top[j : j + 1, :]
    for j in range(8):
        new = jnp.where(lane == at + j, cols[j], new)
    rest = jnp.where((lane >= at) & (lane < at + 8), 0.0, other)
    for j in range(8):
        rest = rest - other[:, at + j : at + j + 1] * new[j : j + 1, :]
    return new, rest


def sweep(mats, start, stop):
    lane = lax.broadcasted_iota(jnp.int32, (8, 128), 1)
    sub = lax.broadcasted_iota(jnp.int32, (8, 128), 0)
    wide = lax.broadcasted_iota(jnp.int32, (NU - 16, 128), 1)

    def body(_, carry):
        out = []
        for mat in carry:
            one, two = eight(mat[:8], mat[8:16], 0, lane, sub)
            two, one = eight(two, one, 8, lane, sub)
            top = jnp.concatenate([one, two], axis=0)
            rest = mat[16:]
            new = jnp.where(wide < 16, 0.0, rest) - jnp.dot(
                rest[:, :16], top, precision=HI, preferred_element_type=jnp.float32
            )
            out.append(pltpu.roll(jnp.concatenate([new, top], axis=0), 112, 1))
        return tuple(out)

    return lax.fori_loop(start, stop, body, mats)


CODE = 32767.0
STEPS = 64.0


def level_kernel(
    leaves, panels, slots_ref, count_ref, child_hbm, panel_hbm, weight_ref, cost_ref, gain_ref,
    child_ref, a_ref, send1, held, send2, mine, ready, land, t_ref,
    high, low, half_sum, part, mate1, mate2, h0, h1, acc0, acc1, acc2, in0, in1, in2, inv_ref,
    ls, lp, as_, ar, cs, cr, es, er,
    m1s, m1r, m2s, m2r, d0s, d0r, d1s, d1r, d2s, d2r, g0s, g0r, g1s, g1r,
):
    leaf = lax.axis_index("leaf")
    own = lax.axis_index("panel")
    stored, row_block, order = child_ref.shape
    par_dev, _, groups = send2.shape[:3]
    slot_count = slots_ref.shape[1]
    chips = panels // 2
    n1, n2 = gain_ref.shape[1], cost_ref.shape[1]
    tiles = order // 128
    half = row_block // 2
    parts = order // 128
    lane = lax.broadcasted_iota(jnp.int32, (1, 128), 1)
    left = lane < 64
    span = held.shape[0] // leaves
    deep = 3 * half

    def offset(j):
        step = (j + 1) // 2
        return step + (leaves - 2 * step) * (1 - lax.rem(j, 2))

    def send(src, dst, ssem, rsem, **to):
        return pltpu.make_async_remote_copy(
            src_ref=src, dst_ref=dst, send_sem=ssem, recv_sem=rsem,
            device_id=to, device_id_type=pl.DeviceIdType.MESH,
        )

    pairs = stored // 2
    loads = [
        pltpu.make_async_copy(child_hbm.at[pl.ds(2 * n, 2)], child_ref.at[pl.ds(2 * n, 2)], ls.at[n])
        for n in range(pairs)
    ]
    load_panel = pltpu.make_async_copy(panel_hbm, a_ref, lp)
    barrier = pltpu.get_barrier_semaphore()

    @pl.loop(1, leaves)
    def _(j):
        pl.semaphore_signal(
            barrier, inc=1, device_id={"leaf": lax.rem(leaf + j, leaves)},
            device_id_type=pl.DeviceIdType.MESH,
        )

    for j in range(1, panels):
        pl.semaphore_signal(
            barrier, inc=1, device_id={"panel": lax.rem(own + j, panels)},
            device_id_type=pl.DeviceIdType.MESH,
        )

    for copy in loads:
        copy.start()
    load_panel.start()

    chip, core = own // 2, own % 2
    upper = chip // (parts // 2)
    side = core + upper - 2 * core * upper

    word_row = lax.broadcasted_iota(jnp.int32, (half, 128), 0)
    word_lane = lax.broadcasted_iota(jnp.int32, (half, 128), 1)
    scale_at = (word_row == 1) & (word_lane == 64 * core)

    def encode(c):
        cols = [pl.ds(pl.multiple_of(lax.rem(chip + t, parts) * 128, 128), 128) for t in range(3)]
        blocks = [child_ref[c, :, at] for at in cols]
        tops = [jnp.max(jnp.abs(x), keepdims=True) for x in blocks]
        top = jnp.maximum(jnp.maximum(tops[0], tops[1]), jnp.maximum(tops[2], 1e-30))
        mark = jnp.floor(jnp.log2(top) * STEPS) + 1.0
        inv = 1.0 / jnp.exp2(mark * (1.0 / STEPS))
        words = []
        for x in blocks:
            x = x * inv
            size = (jnp.sqrt(jnp.abs(x)) * CODE + 0.5).astype(jnp.int32)
            code = jnp.where(x < 0, -size, size)
            words.append(code[:half] * 65536 + (code[half:] & 65535))
        words[0] = jnp.where(scale_at, mark.astype(jnp.int32), words[0])
        for t in range(2):
            send1[pl.ds(t * stored + c, half, stride=span), :] = words[t]
        return words[2]

    @pl.loop(0, pairs)
    def _(n):
        pltpu.make_async_copy(
            child_hbm.at[pl.ds(2 * n, 2)], child_ref.at[pl.ds(2 * n, 2)], ls.at[n]
        ).wait()
        even, odd = encode(2 * n), encode(2 * n + 1)
        even = jnp.where(side == 0, even, pltpu.roll(even, 64, 1))
        odd = jnp.where(side == 1, odd, pltpu.roll(odd, 64, 1))
        send1[pl.ds(2 * stored + n, half, stride=span), :] = jnp.where(left, even, odd)

    pl.semaphore_wait(barrier, leaves + panels - 2)

    def message(i):
        return pl.ds(pl.multiple_of(i * span, 8), span)

    def piece(j, source):
        to = lax.rem(leaf + offset(j), leaves)
        return send(
            send1.at[message(to)], held.at[message(source)],
            as_.at[j - 1], ar.at[j - 1], leaf=to,
        )

    def source_of(j):
        return lax.rem(leaf + leaves - offset(j), leaves)

    @pl.loop(1, leaves)
    def _(j):
        piece(j, leaf).start()

    held[message(leaf), :] = send1[message(leaf), :]

    @pl.loop(1, leaves)
    def _(j):
        piece(j, source_of(j)).wait_recv()

    def parcel(p, j, source):
        to = lax.rem(leaf + offset(j), leaves)
        return send(
            send2.at[p, to], mine.at[p, source], cs.at[p, j - 1], cr.at[p, j - 1], leaf=to
        )

    def collect(p, d):
        children = [slots_ref[d * par_dev + p, k] for k in range(slot_count)]
        firsts = [lax.shift_right_logical(c, 4) * span for c in children]
        locals_ = [c & (stored - 1) for c in children]
        for t in range(2):
            for k in range(slot_count):
                row = held[pl.ds(firsts[k] + locals_[k] + t * stored, 1), :]
                at = t * slot_count + k
                send2[p, d, at // 4, at % 4 : at % 4 + 1, :] = row
        for n in range(slot_count // 2):
            pick = []
            for e in range(2):
                k = 2 * n + e
                row = held[
                    pl.ds(firsts[k] + 2 * stored + lax.shift_right_logical(locals_[k], 1), 1), :
                ]
                pick.append(jnp.where((locals_[k] & 1) == e, row, pltpu.roll(row, 64, 1)))
            at = 2 * slot_count + n
            send2[p, d, at // 4, at % 4 : at % 4 + 1, :] = jnp.where(left, pick[0], pick[1])

    for p in range(par_dev):

        @pl.loop(1, leaves)
        def _(j):
            collect(p, lax.rem(leaf + offset(j), leaves))
            parcel(p, j, leaf).start()

        collect(p, leaf)
        mine[p, leaf] = send2[p, leaf]

    def slot(p, j, source):
        to = lax.rem(own + j, panels)
        at = pl.ds(pl.multiple_of((p * slot_count + to) * deep, 8), deep)
        return send(
            ready.at[at], land.at[p, source], es.at[p, j - 1], er.at[p, j - 1], panel=to
        )

    def from_of(j):
        return lax.rem(own + panels - j, panels)

    for p in range(par_dev):

        @pl.loop(1, leaves)
        def _(j):
            parcel(p, j, source_of(j)).wait_recv()

        @pl.loop(0, leaves)
        def _(i):
            base = p * slot_count * deep + i
            for t in range(2):
                for g in range(slot_count // 4):
                    at = base + g * 4 * deep + t * half
                    ready[pl.ds(at, 4, stride=deep), :] = mine[p, i, t * slot_count // 4 + g]
            for g in range(slot_count // 8):
                row = mine[p, i, slot_count // 2 + g]
                for e in range(2):
                    at = base + (g * 8 + e) * deep + 2 * half
                    ready[pl.ds(at, 4, stride=2 * deep), :] = row

        for j in range(1, panels):
            slot(p, j, own).start()
        land[p, own] = ready[
            pl.ds(pl.multiple_of((p * slot_count + own) * deep, 8), deep), :
        ]

    def weights(n, q):
        first_lane = 64 * (q % 2)
        gain = jnp.where((word_row == 1) & (word_lane == first_lane), 0.0, 0.5)
        if n == 0:
            lone = (word_lane == first_lane + 1) | (word_lane == first_lane + 1 + half)
            gain = jnp.where((word_row == 0) & lone, 1.0, gain)
        return gain

    factor = [[weights(n, q) for n in range(2)] for q in range(2)]

    def decode(p, q):
        mark = land[p, q, 1:2, 64 * (q % 2) : 64 * (q % 2) + 1].astype(jnp.float32)
        scale = jnp.exp2(mark * (1.0 / STEPS)) * (1.0 / (CODE * CODE))
        scale = jnp.where(own < count_ref[leaf * par_dev + p], scale, 0.0)
        for t in range(4):
            for n in range(2):
                if t < 3:
                    word = land[p, q, t * half : t * half + half, :]
                    code = word >> 16 if n == 0 else (word << 16) >> 16
                    v = code.astype(jnp.float32)
                    v = v * jnp.abs(v) * scale
                    if t == 0:
                        v = v * factor[q % 2][n]
                    if t == 2:
                        q_side = (q % 2) ^ (q // 2 // (parts // 2))
                        v = jnp.where(core == q_side, v, pltpu.roll(v, 64, 1))
                        v = jnp.where(left if q_side == 0 else ~left, v, 0.0)
                    hi = v.astype(jnp.bfloat16)
                    lo = (v - hi.astype(jnp.float32)).astype(jnp.bfloat16)
                else:
                    hi = lo = jnp.zeros((half, 128), jnp.bfloat16)
                at = (q // 2 + t) % parts * 128
                row = q * row_block + n * half
                t_ref[p, row : row + half, at : at + 128] = hi
                t_ref[p, order + row : order + row + half, at : at + 128] = lo

    load_panel.wait()
    for p in range(par_dev):
        for j in range(1, panels):
            slot(p, j, from_of(j)).wait_recv()
        for q in range(panels):
            decode(p, q)

        @pl.loop(0, tiles)
        def _(i):
            rows = pl.ds(pl.multiple_of(i * 128, 128), 128)
            low_rows = pl.ds(pl.multiple_of(order + i * 128, 128), 128)
            a = a_ref[p]
            prod = jnp.dot(t_ref[p, rows, :], a, preferred_element_type=jnp.float32)
            prod = prod + jnp.dot(t_ref[p, low_rows, :], a, preferred_element_type=jnp.float32)
            top = prod.astype(jnp.bfloat16)
            high[p, rows, :] = top
            low[p, rows, :] = (prod - top.astype(jnp.float32)).astype(jnp.bfloat16)

        @pl.loop(0, tiles)
        def _(i):
            rows = pl.ds(pl.multiple_of(i * 128, 128), 128)
            a = a_ref[p, :, rows]
            total = [
                lax.dot_general(
                    a, x[p], (((0,), (0,)), ((), ())), preferred_element_type=jnp.float32
                )
                for x in (high, low)
            ]
            half_sum[p, rows, :] = total[0] + total[1]

    mate = 2 * chip + 1 - core

    def mirror(p, i):
        rows = slice(i * 128, i * 128 + 128)
        for j in range(tiles):
            cols = slice(j * 128, j * 128 + 128)
            part[p, rows, cols] = half_sum[p, rows, cols] + half_sum[p, cols, rows].T

    def rows1(t, c):
        return pl.ds(pl.multiple_of((2 * t + c) * n1, 8), n1)

    def rows2(t, c):
        return pl.ds(pl.multiple_of(NU + (2 * t + c) * n2, 8), n2)

    first = [
        send(part.at[:, rows1(t, 1 - core), :], mate1.at[t], m1s.at[t], m1r.at[t], panel=mate)
        for t in range(chips)
    ]
    second = [
        send(part.at[:, rows2(t, 1 - core), NU:], mate2.at[t], m2s.at[t], m2r.at[t], panel=mate)
        for t in range(chips)
    ]
    for p in range(par_dev):
        mirror(p, 0)
    for copy in first:
        copy.start()
    for p in range(par_dev):
        for i in range(1, tiles):
            mirror(p, i)
    for copy in second:
        copy.start()
    others = [lax.rem(chip + j, chips) for j in range(1, chips)]

    def spread(acc, land, ssem, rsem):
        return [
            send(acc.at[o], land.at[j], ssem.at[j], rsem.at[j], panel=2 * o + core)
            for j, o in enumerate(others)
        ]

    def gathered(ref, ssem, rsem, source):
        return [
            send(
                ref.at[at], ref.at[at], ssem.at[j - 1], rsem.at[j - 1],
                panel=lax.rem(own + j, panels),
            )
            for j, at in ((j, source(j)) for j in range(1, panels))
        ]

    def summed(acc, land):
        total = acc[chip]
        for j in range(chips - 1):
            total = total + land[j]
        return total

    for t in range(chips):
        first[t].wait_recv()
        acc0[t] = part[:, rows1(t, core), :NU] + mate1[t, :, :, :NU]
    out0 = spread(acc0, in0, d0s, d0r)
    for copy in out0:
        copy.start()
    for t in range(chips):
        acc1[t] = part[:, rows1(t, core), NU:] + mate1[t, :, :, NU:]
    out1 = spread(acc1, in1, d1s, d1r)
    for copy in out1:
        copy.start()
    for copy in out0:
        copy.wait_recv()
    h0[own] = summed(acc0, in0)
    share0 = gathered(h0, g0s, g0r, lambda j: own)
    for copy in share0:
        copy.start()
    for t in range(chips):
        second[t].wait_recv()
        acc2[t] = part[:, rows2(t, core), NU:] + mate2[t]
    for copy in out1:
        copy.wait_recv()
    h1[own] = summed(acc1, in1)
    share1 = gathered(h1, g1s, g1r, lambda j: own)
    for copy in share1:
        copy.start()
    out2 = spread(acc2, in2, d2s, d2r)
    for copy in out2:
        copy.start()
    for copy in gathered(h0, g0s, g0r, lambda j: lax.rem(own + panels - j, panels)):
        copy.wait_recv()

    row = lax.broadcasted_iota(jnp.int32, (NU, NU), 0)
    col = lax.broadcasted_iota(jnp.int32, (NU, NU), 1)
    mats = []
    for p in range(par_dev):
        mat = jnp.concatenate([h0[q, p] for q in range(panels)], axis=0)
        mats.append(mat + jnp.where(row == col, weight_ref[p : p + 1, :NU], 0.0))
    mats = sweep(tuple(mats), 0, NU // 16)
    for p in range(par_dev):
        inv_ref[p] = mats[p]
    for copy in gathered(h1, g1s, g1r, lambda j: lax.rem(own + panels - j, panels)):
        copy.wait_recv()
    width = order - NU
    on_diag = lax.broadcasted_iota(jnp.int32, (n2, width), 1) == (
        lax.broadcasted_iota(jnp.int32, (n2, width), 0) + own * n2
    )
    pick = jnp.where(on_diag, 1.0, 0.0)
    product = functools.partial(
        lax.dot_general, precision=HI, preferred_element_type=jnp.float32
    )
    taken = []
    for p in range(par_dev):
        cross = jnp.concatenate([h1[q, p] for q in range(panels)], axis=0)
        own_rows = inv_ref[p, pl.ds(pl.multiple_of(own * n1, 8), n1), :]
        gain_ref[p] = -product(own_rows, cross, (((1,), (0,)), ((), ())))
        own_cross = product(pick, cross, (((1,), (1,)), ((), ())))
        lead = product(own_cross, inv_ref[p], (((1,), (0,)), ((), ())))
        taken.append(product(lead, cross, (((1,), (0,)), ((), ()))))
    for copy in out2:
        copy.wait_recv()
    for p in range(par_dev):
        total = acc2[chip, p]
        for j in range(chips - 1):
            total = total + in2[j, p]
        cost_ref[p] = (
            total + jnp.where(on_diag, weight_ref[p : p + 1, NU:], 0.0) - taken[p]
        )
    for copy in first + second + out0 + out1 + out2 + share0 + share1:
        copy.wait_send()

    @pl.loop(1, leaves)
    def _(j):
        piece(j, leaf).wait_send()
        for p in range(par_dev):
            parcel(p, j, leaf).wait_send()

    for j in range(1, panels):
        for p in range(par_dev):
            slot(p, j, own).wait_send()


def level(child_cost, panel, section_weight, parent_slots, child_count, leaves, panels):
    stored, row_block, order = child_cost.shape
    parents, slot_count = parent_slots.shape
    par_dev = parents // leaves
    chips = panels // 2
    half = row_block // 2
    rows = stored * 5 // 2
    groups = slot_count * 5 // 8
    n1, n2 = NU // panels, (order - NU) // panels
    zero, one, two = (par_dev, n1, NU), (par_dev, n1, order - NU), (par_dev, n2, order - NU)
    vmem = pl.BlockSpec(memory_space=pltpu.VMEM)
    smem = pl.BlockSpec(memory_space=pltpu.SMEM)
    hbm = pl.BlockSpec(memory_space=pltpu.HBM)
    dma = pltpu.SemaphoreType.DMA
    word = lambda *shape: pltpu.VMEM(shape + (128,), jnp.int32)
    f32 = lambda *shape: pltpu.VMEM(shape, jnp.float32)
    b16 = lambda *shape: pltpu.VMEM(shape, jnp.bfloat16)
    return pl.pallas_call(
        functools.partial(level_kernel, leaves, panels),
        out_shape=(
            jax.ShapeDtypeStruct((par_dev, n2, order - NU), jnp.float32),
            jax.ShapeDtypeStruct((par_dev, n1, order - NU), jnp.float32),
        ),
        in_specs=[smem, smem, hbm, hbm, vmem],
        out_specs=(vmem, vmem),
        scratch_shapes=[
            f32(stored, row_block, order),
            b16(par_dev, order, order),
            word(leaves * rows),
            word(leaves * rows),
            word(par_dev, leaves, groups, 4),
            word(par_dev, leaves, groups, 4),
            word(par_dev * slot_count * 3 * half),
            word(par_dev, panels, 3 * half),
            b16(par_dev, 2 * order, order),
            b16(par_dev, order, order),
            b16(par_dev, order, order),
            f32(par_dev, order, order),
            f32(par_dev, order, order),
            f32(chips, par_dev, n1, order),
            f32(chips, *two),
            f32(panels, *zero),
            f32(panels, *one),
            f32(chips, *zero),
            f32(chips, *one),
            f32(chips, *two),
            f32(chips - 1, *zero),
            f32(chips - 1, *one),
            f32(chips - 1, *two),
            f32(par_dev, NU, NU),
            dma((stored // 2,)),
            dma,
        ]
        + [dma((leaves - 1,))] * 2
        + [dma((par_dev, leaves - 1))] * 2
        + [dma((par_dev, panels - 1))] * 2
        + [dma((chips,))] * 4
        + [dma((chips - 1,))] * 6
        + [dma((panels - 1,))] * 4,
        compiler_params=pltpu.CompilerParams(
            collective_id=0, has_side_effects=True, vmem_limit_bytes=56 << 20
        ),
        name="level",
    )(parent_slots, child_count, child_cost, panel, section_weight)


def per_device(child_cost, panel, section_weight, parent_slots, child_count):
    leaves = lax.axis_size("leaf")
    panels = lax.axis_size("panel")
    return level(child_cost, panel, section_weight, parent_slots, child_count, leaves, panels)


def solution(mesh):
    in_specs = (P("leaf", "panel", None), P("leaf", "panel", None), P("leaf", None), P(), P())
    out_specs = (P("leaf", "panel", None), P("leaf", "panel", None))
    return jax.shard_map(
        per_device, mesh=mesh, in_specs=in_specs, out_specs=out_specs, check_vma=False
    )
```

```python
import functools

import jax
import jax.numpy as jnp
from jax import lax
from jax.experimental import pallas as pl
from jax.experimental.pallas import tpu as pltpu
from jax.sharding import PartitionSpec as P

NU = 128
HI = lax.Precision.HIGHEST


def pivots(cols, sub):
    for k in range(8):
        inv = 1.0 / jnp.broadcast_to(cols[k][k : k + 1, :], (8, 128))
        rows = [inv if j == k else c[k : k + 1, :] * inv for j, c in enumerate(cols)]
        pivot = cols[k]
        cols = [
            jnp.where(sub == k, rows[j], (0.0 if j == k else c) - pivot * rows[j])
            for j, c in enumerate(cols)
        ]
    return cols


def eight(top, other, at, lane, sub):
    cols = [jnp.broadcast_to(top[:, at + j : at + j + 1], (8, 128)) for j in range(8)]
    cols = pivots(cols, sub)
    new = cols[0] * top[0:1, :]
    for j in range(1, 8):
        new = new + cols[j] * top[j : j + 1, :]
    for j in range(8):
        new = jnp.where(lane == at + j, cols[j], new)
    rest = jnp.where((lane >= at) & (lane < at + 8), 0.0, other)
    for j in range(8):
        rest = rest - other[:, at + j : at + j + 1] * new[j : j + 1, :]
    return new, rest


def sweep(mats, start, stop):
    lane = lax.broadcasted_iota(jnp.int32, (8, 128), 1)
    sub = lax.broadcasted_iota(jnp.int32, (8, 128), 0)
    wide = lax.broadcasted_iota(jnp.int32, (NU - 16, 128), 1)

    def body(_, carry):
        out = []
        for mat in carry:
            one, two = eight(mat[:8], mat[8:16], 0, lane, sub)
            two, one = eight(two, one, 8, lane, sub)
            top = jnp.concatenate([one, two], axis=0)
            rest = mat[16:]
            new = jnp.where(wide < 16, 0.0, rest) - jnp.dot(
                rest[:, :16], top, precision=HI, preferred_element_type=jnp.float32
            )
            out.append(pltpu.roll(jnp.concatenate([new, top], axis=0), 112, 1))
        return tuple(out)

    return lax.fori_loop(start, stop, body, mats)


CODE = 32767.0
STEPS = 64.0


def level_kernel(
    leaves, panels, slots_ref, count_ref, child_hbm, panel_hbm, weight_ref, cost_ref, gain_ref,
    child_ref, a_ref, send1, held, send2, mine, ready, land, t_ref,
    high, low, half_sum, part, mate1, mate2, h0, h1, acc0, acc1, acc2, in0, in1, in2, inv_ref,
    ls, lp, as_, ar, cs, cr, es, er,
    m1s, m1r, m2s, m2r, d0s, d0r, d1s, d1r, d2s, d2r, g0s, g0r, g1s, g1r,
):
    leaf = lax.axis_index("leaf")
    own = lax.axis_index("panel")
    stored, row_block, order = child_ref.shape
    par_dev, _, groups = send2.shape[:3]
    slot_count = slots_ref.shape[0]
    chips = panels // 2
    n1, n2 = gain_ref.shape[1], cost_ref.shape[1]
    tiles = order // 128
    half = row_block // 2
    parts = order // 128
    lane = lax.broadcasted_iota(jnp.int32, (1, 128), 1)
    left = lane < 64
    span = held.shape[0] // leaves
    deep = 3 * half

    def offset(j):
        step = (j + 1) // 2
        return step + (leaves - 2 * step) * (1 - lax.rem(j, 2))

    def send(src, dst, ssem, rsem, **to):
        return pltpu.make_async_remote_copy(
            src_ref=src, dst_ref=dst, send_sem=ssem, recv_sem=rsem,
            device_id=to, device_id_type=pl.DeviceIdType.MESH,
        )

    pairs = stored // 2
    loads = [
        pltpu.make_async_copy(child_hbm.at[pl.ds(2 * n, 2)], child_ref.at[pl.ds(2 * n, 2)], ls.at[n])
        for n in range(pairs)
    ]
    load_panel = pltpu.make_async_copy(panel_hbm, a_ref, lp)
    barrier = pltpu.get_barrier_semaphore()

    @pl.loop(1, leaves)
    def _(j):
        pl.semaphore_signal(
            barrier, inc=1, device_id={"leaf": lax.rem(leaf + j, leaves)},
            device_id_type=pl.DeviceIdType.MESH,
        )

    for j in range(1, panels):
        pl.semaphore_signal(
            barrier, inc=1, device_id={"panel": lax.rem(own + j, panels)},
            device_id_type=pl.DeviceIdType.MESH,
        )

    for copy in loads:
        copy.start()
    load_panel.start()

    chip, core = own // 2, own % 2
    upper = chip // (parts // 2)
    side = core + upper - 2 * core * upper

    word_row = lax.broadcasted_iota(jnp.int32, (half, 128), 0)
    word_lane = lax.broadcasted_iota(jnp.int32, (half, 128), 1)
    scale_at = (word_row == 1) & (word_lane == 64 * core)

    def encode(c):
        cols = [pl.ds(pl.multiple_of(lax.rem(chip + t, parts) * 128, 128), 128) for t in range(3)]
        blocks = [child_ref[c, :, at] for at in cols]
        tops = [jnp.max(jnp.abs(x), keepdims=True) for x in blocks]
        top = jnp.maximum(jnp.maximum(tops[0], tops[1]), jnp.maximum(tops[2], 1e-30))
        mark = jnp.floor(jnp.log2(top) * STEPS) + 1.0
        inv = 1.0 / jnp.exp2(mark * (1.0 / STEPS))
        words = []
        for x in blocks:
            x = x * inv
            size = (jnp.sqrt(jnp.abs(x)) * CODE + 0.5).astype(jnp.int32)
            code = jnp.where(x < 0, -size, size)
            words.append(code[:half] * 65536 + (code[half:] & 65535))
        words[0] = jnp.where(scale_at, mark.astype(jnp.int32), words[0])
        for t in range(2):
            send1[pl.ds(t * stored + c, half, stride=span), :] = words[t]
        return words[2]

    @pl.loop(0, pairs)
    def _(n):
        pltpu.make_async_copy(
            child_hbm.at[pl.ds(2 * n, 2)], child_ref.at[pl.ds(2 * n, 2)], ls.at[n]
        ).wait()
        even, odd = encode(2 * n), encode(2 * n + 1)
        even = jnp.where(side == 0, even, pltpu.roll(even, 64, 1))
        odd = jnp.where(side == 1, odd, pltpu.roll(odd, 64, 1))
        send1[pl.ds(2 * stored + n, half, stride=span), :] = jnp.where(left, even, odd)

    pl.semaphore_wait(barrier, leaves + panels - 2)

    def message(i):
        return pl.ds(pl.multiple_of(i * span, 8), span)

    def piece(j, source):
        to = lax.rem(leaf + offset(j), leaves)
        return send(
            send1.at[message(to)], held.at[message(source)],
            as_.at[j - 1], ar.at[j - 1], leaf=to,
        )

    def source_of(j):
        return lax.rem(leaf + leaves - offset(j), leaves)

    @pl.loop(1, leaves)
    def _(j):
        piece(j, leaf).start()

    held[message(leaf), :] = send1[message(leaf), :]

    @pl.loop(1, leaves)
    def _(j):
        piece(j, source_of(j)).wait_recv()

    def parcel(p, j, source):
        to = lax.rem(leaf + offset(j), leaves)
        return send(
            send2.at[p, to], mine.at[p, source], cs.at[p, j - 1], cr.at[p, j - 1], leaf=to
        )

    def collect(p, d):
        children = [slots_ref[k, d * par_dev + p] for k in range(slot_count)]
        firsts = [lax.shift_right_logical(c, 4) * span for c in children]
        locals_ = [c & (stored - 1) for c in children]
        for t in range(2):
            for k in range(slot_count):
                row = held[pl.ds(firsts[k] + locals_[k] + t * stored, 1), :]
                at = t * slot_count + k
                send2[p, d, at // 4, at % 4 : at % 4 + 1, :] = row
        for n in range(slot_count // 2):
            pick = []
            for e in range(2):
                k = 2 * n + e
                row = held[
                    pl.ds(firsts[k] + 2 * stored + lax.shift_right_logical(locals_[k], 1), 1), :
                ]
                pick.append(jnp.where((locals_[k] & 1) == e, row, pltpu.roll(row, 64, 1)))
            at = 2 * slot_count + n
            send2[p, d, at // 4, at % 4 : at % 4 + 1, :] = jnp.where(left, pick[0], pick[1])

    for p in range(par_dev):

        @pl.loop(1, leaves)
        def _(j):
            collect(p, lax.rem(leaf + offset(j), leaves))
            parcel(p, j, leaf).start()

        collect(p, leaf)
        mine[p, leaf] = send2[p, leaf]

    def slot(p, j, source):
        to = lax.rem(own + j, panels)
        at = pl.ds(pl.multiple_of((p * slot_count + to) * deep, 8), deep)
        return send(
            ready.at[at], land.at[p, source], es.at[p, j - 1], er.at[p, j - 1], panel=to
        )

    def from_of(j):
        return lax.rem(own + panels - j, panels)

    for p in range(par_dev):

        @pl.loop(1, leaves)
        def _(j):
            parcel(p, j, source_of(j)).wait_recv()

        @pl.loop(0, leaves)
        def _(i):
            base = p * slot_count * deep + i
            for t in range(2):
                for g in range(slot_count // 4):
                    at = base + g * 4 * deep + t * half
                    ready[pl.ds(at, 4, stride=deep), :] = mine[p, i, t * slot_count // 4 + g]
            for g in range(slot_count // 8):
                row = mine[p, i, slot_count // 2 + g]
                for e in range(2):
                    at = base + (g * 8 + e) * deep + 2 * half
                    ready[pl.ds(at, 4, stride=2 * deep), :] = row

        for j in range(1, panels):
            slot(p, j, own).start()
        land[p, own] = ready[
            pl.ds(pl.multiple_of((p * slot_count + own) * deep, 8), deep), :
        ]

    def weights(n, q):
        first_lane = 64 * (q % 2)
        gain = jnp.where((word_row == 1) & (word_lane == first_lane), 0.0, 0.5)
        if n == 0:
            lone = (word_lane == first_lane + 1) | (word_lane == first_lane + 1 + half)
            gain = jnp.where((word_row == 0) & lone, 1.0, gain)
        return gain

    factor = [[weights(n, q) for n in range(2)] for q in range(2)]

    def decode(p, q):
        mark = land[p, q, 1:2, 64 * (q % 2) : 64 * (q % 2) + 1].astype(jnp.float32)
        scale = jnp.exp2(mark * (1.0 / STEPS)) * (1.0 / (CODE * CODE))
        scale = jnp.where(own < count_ref[leaf * par_dev + p], scale, 0.0)
        for t in range(4):
            for n in range(2):
                if t < 3:
                    word = land[p, q, t * half : t * half + half, :]
                    code = word >> 16 if n == 0 else (word << 16) >> 16
                    v = code.astype(jnp.float32)
                    v = v * jnp.abs(v) * scale
                    if t == 0:
                        v = v * factor[q % 2][n]
                    if t == 2:
                        q_side = (q % 2) ^ (q // 2 // (parts // 2))
                        v = jnp.where(core == q_side, v, pltpu.roll(v, 64, 1))
                        v = jnp.where(left if q_side == 0 else ~left, v, 0.0)
                    hi = v.astype(jnp.bfloat16)
                    lo = (v - hi.astype(jnp.float32)).astype(jnp.bfloat16)
                else:
                    hi = lo = jnp.zeros((half, 128), jnp.bfloat16)
                at = (q // 2 + t) % parts * 128
                row = q * row_block + n * half
                t_ref[p, row : row + half, at : at + 128] = hi
                t_ref[p, order + row : order + row + half, at : at + 128] = lo

    load_panel.wait()
    for p in range(par_dev):
        for j in range(1, panels):
            slot(p, j, from_of(j)).wait_recv()
        for q in range(panels):
            decode(p, q)

        @pl.loop(0, tiles)
        def _(i):
            rows = pl.ds(pl.multiple_of(i * 128, 128), 128)
            low_rows = pl.ds(pl.multiple_of(order + i * 128, 128), 128)
            a = a_ref[p]
            prod = jnp.dot(t_ref[p, rows, :], a, preferred_element_type=jnp.float32)
            prod = prod + jnp.dot(t_ref[p, low_rows, :], a, preferred_element_type=jnp.float32)
            top = prod.astype(jnp.bfloat16)
            high[p, rows, :] = top
            low[p, rows, :] = (prod - top.astype(jnp.float32)).astype(jnp.bfloat16)

        @pl.loop(0, tiles)
        def _(i):
            rows = pl.ds(pl.multiple_of(i * 128, 128), 128)
            a = a_ref[p, :, rows]
            total = [
                lax.dot_general(
                    a, x[p], (((0,), (0,)), ((), ())), preferred_element_type=jnp.float32
                )
                for x in (high, low)
            ]
            half_sum[p, rows, :] = total[0] + total[1]

    mate = 2 * chip + 1 - core

    def mirror(p, i):
        rows = slice(i * 128, i * 128 + 128)
        for j in range(tiles):
            cols = slice(j * 128, j * 128 + 128)
            part[p, rows, cols] = half_sum[p, rows, cols] + half_sum[p, cols, rows].T

    def rows1(t, c):
        return pl.ds(pl.multiple_of((2 * t + c) * n1, 8), n1)

    def rows2(t, c):
        return pl.ds(pl.multiple_of(NU + (2 * t + c) * n2, 8), n2)

    first = [
        send(part.at[:, rows1(t, 1 - core), :], mate1.at[t], m1s.at[t], m1r.at[t], panel=mate)
        for t in range(chips)
    ]
    second = [
        send(part.at[:, rows2(t, 1 - core), NU:], mate2.at[t], m2s.at[t], m2r.at[t], panel=mate)
        for t in range(chips)
    ]
    for p in range(par_dev):
        mirror(p, 0)
    for copy in first:
        copy.start()
    for p in range(par_dev):
        for i in range(1, tiles):
            mirror(p, i)
    for copy in second:
        copy.start()
    others = [lax.rem(chip + j, chips) for j in range(1, chips)]

    def spread(acc, land, ssem, rsem):
        return [
            send(acc.at[o], land.at[j], ssem.at[j], rsem.at[j], panel=2 * o + core)
            for j, o in enumerate(others)
        ]

    def gathered(ref, ssem, rsem, source):
        return [
            send(
                ref.at[at], ref.at[at], ssem.at[j - 1], rsem.at[j - 1],
                panel=lax.rem(own + j, panels),
            )
            for j, at in ((j, source(j)) for j in range(1, panels))
        ]

    def summed(acc, land):
        total = acc[chip]
        for j in range(chips - 1):
            total = total + land[j]
        return total

    for t in range(chips):
        first[t].wait_recv()
        acc0[t] = part[:, rows1(t, core), :NU] + mate1[t, :, :, :NU]
    out0 = spread(acc0, in0, d0s, d0r)
    for copy in out0:
        copy.start()
    for t in range(chips):
        acc1[t] = part[:, rows1(t, core), NU:] + mate1[t, :, :, NU:]
    out1 = spread(acc1, in1, d1s, d1r)
    for copy in out1:
        copy.start()
    for copy in out0:
        copy.wait_recv()
    h0[own] = summed(acc0, in0)
    share0 = gathered(h0, g0s, g0r, lambda j: own)
    for copy in share0:
        copy.start()
    for t in range(chips):
        second[t].wait_recv()
        acc2[t] = part[:, rows2(t, core), NU:] + mate2[t]
    for copy in out1:
        copy.wait_recv()
    h1[own] = summed(acc1, in1)
    share1 = gathered(h1, g1s, g1r, lambda j: own)
    for copy in share1:
        copy.start()
    out2 = spread(acc2, in2, d2s, d2r)
    for copy in out2:
        copy.start()
    for copy in gathered(h0, g0s, g0r, lambda j: lax.rem(own + panels - j, panels)):
        copy.wait_recv()

    row = lax.broadcasted_iota(jnp.int32, (NU, NU), 0)
    col = lax.broadcasted_iota(jnp.int32, (NU, NU), 1)
    mats = []
    for p in range(par_dev):
        mat = jnp.concatenate([h0[q, p] for q in range(panels)], axis=0)
        mats.append(mat + jnp.where(row == col, weight_ref[p : p + 1, :NU], 0.0))
    mats = sweep(tuple(mats), 0, NU // 16)
    for p in range(par_dev):
        inv_ref[p] = mats[p]
    for copy in gathered(h1, g1s, g1r, lambda j: lax.rem(own + panels - j, panels)):
        copy.wait_recv()
    width = order - NU
    on_diag = lax.broadcasted_iota(jnp.int32, (n2, width), 1) == (
        lax.broadcasted_iota(jnp.int32, (n2, width), 0) + own * n2
    )
    pick = jnp.where(on_diag, 1.0, 0.0)
    product = functools.partial(
        lax.dot_general, precision=HI, preferred_element_type=jnp.float32
    )
    taken = []
    for p in range(par_dev):
        cross = jnp.concatenate([h1[q, p] for q in range(panels)], axis=0)
        own_rows = inv_ref[p, pl.ds(pl.multiple_of(own * n1, 8), n1), :]
        gain_ref[p] = -product(own_rows, cross, (((1,), (0,)), ((), ())))
        own_cross = product(pick, cross, (((1,), (1,)), ((), ())))
        lead = product(own_cross, inv_ref[p], (((1,), (0,)), ((), ())))
        taken.append(product(lead, cross, (((1,), (0,)), ((), ()))))
    for copy in out2:
        copy.wait_recv()
    for p in range(par_dev):
        total = acc2[chip, p]
        for j in range(chips - 1):
            total = total + in2[j, p]
        cost_ref[p] = (
            total + jnp.where(on_diag, weight_ref[p : p + 1, NU:], 0.0) - taken[p]
        )
    for copy in first + second + out0 + out1 + out2 + share0 + share1:
        copy.wait_send()

    @pl.loop(1, leaves)
    def _(j):
        piece(j, leaf).wait_send()
        for p in range(par_dev):
            parcel(p, j, leaf).wait_send()

    for j in range(1, panels):
        for p in range(par_dev):
            slot(p, j, own).wait_send()


def level(child_cost, panel, section_weight, parent_slots, child_count, leaves, panels):
    stored, row_block, order = child_cost.shape
    parents, slot_count = parent_slots.shape
    par_dev = parents // leaves
    chips = panels // 2
    half = row_block // 2
    rows = stored * 5 // 2
    groups = slot_count * 5 // 8
    n1, n2 = NU // panels, (order - NU) // panels
    zero, one, two = (par_dev, n1, NU), (par_dev, n1, order - NU), (par_dev, n2, order - NU)
    vmem = pl.BlockSpec(memory_space=pltpu.VMEM)
    smem = pl.BlockSpec(memory_space=pltpu.SMEM)
    hbm = pl.BlockSpec(memory_space=pltpu.HBM)
    dma = pltpu.SemaphoreType.DMA
    word = lambda *shape: pltpu.VMEM(shape + (128,), jnp.int32)
    f32 = lambda *shape: pltpu.VMEM(shape, jnp.float32)
    b16 = lambda *shape: pltpu.VMEM(shape, jnp.bfloat16)
    return pl.pallas_call(
        functools.partial(level_kernel, leaves, panels),
        out_shape=(
            jax.ShapeDtypeStruct((par_dev, n2, order - NU), jnp.float32),
            jax.ShapeDtypeStruct((par_dev, n1, order - NU), jnp.float32),
        ),
        in_specs=[smem, smem, hbm, hbm, vmem],
        out_specs=(vmem, vmem),
        scratch_shapes=[
            f32(stored, row_block, order),
            b16(par_dev, order, order),
            word(leaves * rows),
            word(leaves * rows),
            word(par_dev, leaves, groups, 4),
            word(par_dev, leaves, groups, 4),
            word(par_dev * slot_count * 3 * half),
            word(par_dev, panels, 3 * half),
            b16(par_dev, 2 * order, order),
            b16(par_dev, order, order),
            b16(par_dev, order, order),
            f32(par_dev, order, order),
            f32(par_dev, order, order),
            f32(chips, par_dev, n1, order),
            f32(chips, *two),
            f32(panels, *zero),
            f32(panels, *one),
            f32(chips, *zero),
            f32(chips, *one),
            f32(chips, *two),
            f32(chips - 1, *zero),
            f32(chips - 1, *one),
            f32(chips - 1, *two),
            f32(par_dev, NU, NU),
            dma((stored // 2,)),
            dma,
        ]
        + [dma((leaves - 1,))] * 2
        + [dma((par_dev, leaves - 1))] * 2
        + [dma((par_dev, panels - 1))] * 2
        + [dma((chips,))] * 4
        + [dma((chips - 1,))] * 6
        + [dma((panels - 1,))] * 4,
        compiler_params=pltpu.CompilerParams(
            collective_id=0, has_side_effects=True, vmem_limit_bytes=56 << 20
        ),
        name="level",
    )(parent_slots.T, child_count, child_cost, panel, section_weight)


def per_device(child_cost, panel, section_weight, parent_slots, child_count):
    leaves = lax.axis_size("leaf")
    panels = lax.axis_size("panel")
    return level(child_cost, panel, section_weight, parent_slots, child_count, leaves, panels)


def solution(mesh):
    in_specs = (P("leaf", "panel", None), P("leaf", "panel", None), P("leaf", None), P(), P())
    out_specs = (P("leaf", "panel", None), P("leaf", "panel", None))
    return jax.shard_map(
        per_device, mesh=mesh, in_specs=in_specs, out_specs=out_specs, check_vma=False
    )
```

```python
import functools

import jax
import jax.numpy as jnp
from jax import lax
from jax.experimental import pallas as pl
from jax.experimental.pallas import tpu as pltpu
from jax.sharding import PartitionSpec as P

NU = 128
HI = lax.Precision.HIGHEST


def pivots(cols, sub):
    for k in range(8):
        inv = 1.0 / jnp.broadcast_to(cols[k][k : k + 1, :], (8, 128))
        rows = [inv if j == k else c[k : k + 1, :] * inv for j, c in enumerate(cols)]
        pivot = cols[k]
        cols = [
            jnp.where(sub == k, rows[j], (0.0 if j == k else c) - pivot * rows[j])
            for j, c in enumerate(cols)
        ]
    return cols


def eight(top, other, at, lane, sub):
    cols = [jnp.broadcast_to(top[:, at + j : at + j + 1], (8, 128)) for j in range(8)]
    cols = pivots(cols, sub)
    new = cols[0] * top[0:1, :]
    for j in range(1, 8):
        new = new + cols[j] * top[j : j + 1, :]
    for j in range(8):
        new = jnp.where(lane == at + j, cols[j], new)
    rest = jnp.where((lane >= at) & (lane < at + 8), 0.0, other)
    for j in range(8):
        rest = rest - other[:, at + j : at + j + 1] * new[j : j + 1, :]
    return new, rest


def sweep(mats, start, stop):
    lane = lax.broadcasted_iota(jnp.int32, (8, 128), 1)
    sub = lax.broadcasted_iota(jnp.int32, (8, 128), 0)
    wide = lax.broadcasted_iota(jnp.int32, (NU - 16, 128), 1)

    def body(_, carry):
        out = []
        for mat in carry:
            one, two = eight(mat[:8], mat[8:16], 0, lane, sub)
            two, one = eight(two, one, 8, lane, sub)
            top = jnp.concatenate([one, two], axis=0)
            rest = mat[16:]
            new = jnp.where(wide < 16, 0.0, rest) - jnp.dot(
                rest[:, :16], top, precision=HI, preferred_element_type=jnp.float32
            )
            out.append(pltpu.roll(jnp.concatenate([new, top], axis=0), 112, 1))
        return tuple(out)

    return lax.fori_loop(start, stop, body, mats)


CODE = 32767.0
STEPS = 64.0


def level_kernel(
    leaves, panels, slots_ref, count_ref, child_hbm, panel_hbm, weight_ref, cost_ref, gain_ref,
    child_ref, a_ref, send1, held, send2, mine, ready, land, t_ref,
    high, low, half_sum, part, mate1, mate2, h0, h1, acc0, acc1, acc2, in0, in1, in2, inv_ref,
    ls, lp, as_, ar, cs, cr, es, er,
    m1s, m1r, m2s, m2r, d0s, d0r, d1s, d1r, d2s, d2r, g0s, g0r, g1s, g1r,
):
    leaf = lax.axis_index("leaf")
    own = lax.axis_index("panel")
    stored, row_block, order = child_ref.shape
    par_dev, _, groups = send2.shape[:3]
    slot_count = slots_ref.shape[0]
    chips = panels // 2
    n1, n2 = gain_ref.shape[1], cost_ref.shape[1]
    tiles = order // 128
    half = row_block // 2
    parts = order // 128
    lane = lax.broadcasted_iota(jnp.int32, (1, 128), 1)
    left = lane < 64
    span = held.shape[0] // leaves
    deep = 3 * half

    def offset(j):
        step = (j + 1) // 2
        return step + (leaves - 2 * step) * (1 - lax.rem(j, 2))

    def send(src, dst, ssem, rsem, **to):
        return pltpu.make_async_remote_copy(
            src_ref=src, dst_ref=dst, send_sem=ssem, recv_sem=rsem,
            device_id=to, device_id_type=pl.DeviceIdType.MESH,
        )

    pairs = stored // 2
    loads = [
        pltpu.make_async_copy(child_hbm.at[pl.ds(2 * n, 2)], child_ref.at[pl.ds(2 * n, 2)], ls.at[n])
        for n in range(pairs)
    ]
    load_panel = pltpu.make_async_copy(panel_hbm, a_ref, lp)
    barrier = pltpu.get_barrier_semaphore()

    @pl.loop(1, leaves)
    def _(j):
        pl.semaphore_signal(
            barrier, inc=1, device_id={"leaf": lax.rem(leaf + j, leaves)},
            device_id_type=pl.DeviceIdType.MESH,
        )

    for j in range(1, panels):
        pl.semaphore_signal(
            barrier, inc=1, device_id={"panel": lax.rem(own + j, panels)},
            device_id_type=pl.DeviceIdType.MESH,
        )

    for copy in loads:
        copy.start()
    load_panel.start()

    chip, core = own // 2, own % 2
    upper = chip // (parts // 2)
    side = core + upper - 2 * core * upper

    word_row = lax.broadcasted_iota(jnp.int32, (half, 128), 0)
    word_lane = lax.broadcasted_iota(jnp.int32, (half, 128), 1)
    scale_at = (word_row == 1) & (word_lane == 64 * core)

    def encode(c):
        cols = [pl.ds(pl.multiple_of(lax.rem(chip + t, parts) * 128, 128), 128) for t in range(3)]
        blocks = [child_ref[c, :, at] for at in cols]
        tops = [jnp.max(jnp.abs(x), keepdims=True) for x in blocks]
        top = jnp.maximum(jnp.maximum(tops[0], tops[1]), jnp.maximum(tops[2], 1e-30))
        mark = jnp.floor(jnp.log2(top) * STEPS) + 1.0
        inv = 1.0 / jnp.exp2(mark * (1.0 / STEPS))
        words = []
        for x in blocks:
            x = x * inv
            size = (jnp.sqrt(jnp.abs(x)) * CODE + 0.5).astype(jnp.int32)
            code = jnp.where(x < 0, -size, size)
            words.append(code[:half] * 65536 + (code[half:] & 65535))
        words[0] = jnp.where(scale_at, mark.astype(jnp.int32), words[0])
        for t in range(2):
            send1[pl.ds(t * stored + c, half, stride=span), :] = words[t]
        return words[2]

    @pl.loop(0, pairs)
    def _(n):
        pltpu.make_async_copy(
            child_hbm.at[pl.ds(2 * n, 2)], child_ref.at[pl.ds(2 * n, 2)], ls.at[n]
        ).wait()
        even, odd = encode(2 * n), encode(2 * n + 1)
        even = jnp.where(side == 0, even, pltpu.roll(even, 64, 1))
        odd = jnp.where(side == 1, odd, pltpu.roll(odd, 64, 1))
        send1[pl.ds(2 * stored + n, half, stride=span), :] = jnp.where(left, even, odd)

    pl.semaphore_wait(barrier, leaves + panels - 2)

    def message(i):
        return pl.ds(pl.multiple_of(i * span, 8), span)

    def piece(j, source):
        to = lax.rem(leaf + offset(j), leaves)
        return send(
            send1.at[message(to)], held.at[message(source)],
            as_.at[j - 1], ar.at[j - 1], leaf=to,
        )

    def source_of(j):
        return lax.rem(leaf + leaves - offset(j), leaves)

    @pl.loop(1, leaves)
    def _(j):
        piece(j, leaf).start()

    held[message(leaf), :] = send1[message(leaf), :]

    @pl.loop(1, leaves)
    def _(j):
        piece(j, source_of(j)).wait_recv()

    def parcel(p, j, source):
        to = lax.rem(leaf + offset(j), leaves)
        return send(
            send2.at[p, to], mine.at[p, source], cs.at[p, j - 1], cr.at[p, j - 1], leaf=to
        )

    def collect(p, d):
        children = [slots_ref[k, d * par_dev + p] for k in range(slot_count)]
        firsts = [lax.shift_right_logical(c, 4) * span for c in children]
        locals_ = [c & (stored - 1) for c in children]
        for t in range(2):
            for k in range(slot_count):
                row = held[pl.ds(firsts[k] + locals_[k] + t * stored, 1), :]
                at = t * slot_count + k
                send2[p, d, at // 4, at % 4 : at % 4 + 1, :] = row
        for n in range(slot_count // 2):
            pick = []
            for e in range(2):
                k = 2 * n + e
                row = held[
                    pl.ds(firsts[k] + 2 * stored + lax.shift_right_logical(locals_[k], 1), 1), :
                ]
                pick.append(jnp.where((locals_[k] & 1) == e, row, pltpu.roll(row, 64, 1)))
            at = 2 * slot_count + n
            send2[p, d, at // 4, at % 4 : at % 4 + 1, :] = jnp.where(left, pick[0], pick[1])

    for p in range(par_dev):

        @pl.loop(1, leaves)
        def _(j):
            collect(p, lax.rem(leaf + offset(j), leaves))
            parcel(p, j, leaf).start()

        collect(p, leaf)
        mine[p, leaf] = send2[p, leaf]

    def slot(p, j, source):
        to = lax.rem(own + j, panels)
        at = pl.ds(pl.multiple_of((p * slot_count + to) * deep, 8), deep)
        return send(
            ready.at[at], land.at[p, source], es.at[p, j - 1], er.at[p, j - 1], panel=to
        )

    def from_of(j):
        return lax.rem(own + panels - j, panels)

    for p in range(par_dev):

        @pl.loop(1, leaves)
        def _(j):
            parcel(p, j, source_of(j)).wait_recv()

        @pl.loop(0, leaves)
        def _(i):
            base = p * slot_count * deep + i
            for t in range(2):
                for g in range(slot_count // 4):
                    at = base + g * 4 * deep + t * half
                    ready[pl.ds(at, 4, stride=deep), :] = mine[p, i, t * slot_count // 4 + g]
            for g in range(slot_count // 8):
                row = mine[p, i, slot_count // 2 + g]
                for e in range(2):
                    at = base + (g * 8 + e) * deep + 2 * half
                    ready[pl.ds(at, 4, stride=2 * deep), :] = row

        for j in range(1, panels):
            slot(p, j, own).start()
        land[p, own] = ready[
            pl.ds(pl.multiple_of((p * slot_count + own) * deep, 8), deep), :
        ]

    def weights(n, q):
        first_lane = 64 * (q % 2)
        gain = jnp.where((word_row == 1) & (word_lane == first_lane), 0.0, 0.5)
        if n == 0:
            lone = (word_lane == first_lane + 1) | (word_lane == first_lane + 1 + half)
            gain = jnp.where((word_row == 0) & lone, 1.0, gain)
        return gain

    factor = [[weights(n, q) for n in range(2)] for q in range(2)]

    def decode(p, q):
        mark = land[p, q, 1:2, 64 * (q % 2) : 64 * (q % 2) + 1].astype(jnp.float32)
        scale = jnp.exp2(mark * (1.0 / STEPS)) * (1.0 / (CODE * CODE))
        scale = jnp.where(own < count_ref[leaf * par_dev + p], scale, 0.0)
        for t in range(4):
            for n in range(2):
                if t < 3:
                    word = land[p, q, t * half : t * half + half, :]
                    code = word >> 16 if n == 0 else (word << 16) >> 16
                    v = code.astype(jnp.float32)
                    v = v * jnp.abs(v) * scale
                    if t == 0:
                        v = v * factor[q % 2][n]
                    if t == 2:
                        q_side = (q % 2) ^ (q // 2 // (parts // 2))
                        v = jnp.where(core == q_side, v, pltpu.roll(v, 64, 1))
                        v = jnp.where(left if q_side == 0 else ~left, v, 0.0)
                    hi = v.astype(jnp.bfloat16)
                    lo = (v - hi.astype(jnp.float32)).astype(jnp.bfloat16)
                else:
                    hi = lo = jnp.zeros((half, 128), jnp.bfloat16)
                at = (q // 2 + t) % parts * 128
                row = q * row_block + n * half
                t_ref[p, row : row + half, at : at + 128] = hi
                t_ref[p, order + row : order + row + half, at : at + 128] = lo

    load_panel.wait()
    for p in range(par_dev):
        for j in range(1, panels):
            slot(p, j, from_of(j)).wait_recv()
        for q in range(panels):
            decode(p, q)

        @pl.loop(0, tiles)
        def _(i):
            rows = pl.ds(pl.multiple_of(i * 128, 128), 128)
            low_rows = pl.ds(pl.multiple_of(order + i * 128, 128), 128)
            a = a_ref[p]
            prod = jnp.dot(t_ref[p, rows, :], a, preferred_element_type=jnp.float32)
            prod = prod + jnp.dot(t_ref[p, low_rows, :], a, preferred_element_type=jnp.float32)
            top = prod.astype(jnp.bfloat16)
            high[p, rows, :] = top
            low[p, rows, :] = (prod - top.astype(jnp.float32)).astype(jnp.bfloat16)

        @pl.loop(0, tiles)
        def _(i):
            rows = pl.ds(pl.multiple_of(i * 128, 128), 128)
            a = a_ref[p, :, rows]
            total = [
                lax.dot_general(
                    a, x[p], (((0,), (0,)), ((), ())), preferred_element_type=jnp.float32
                )
                for x in (high, low)
            ]
            half_sum[p, rows, :] = total[0] + total[1]

    mate = 2 * chip + 1 - core

    def mirror(p, i):
        rows = slice(i * 128, i * 128 + 128)
        for j in range(tiles):
            cols = slice(j * 128, j * 128 + 128)
            part[p, rows, cols] = half_sum[p, rows, cols] + half_sum[p, cols, rows].T

    def rows1(t, c):
        return pl.ds(pl.multiple_of((2 * t + c) * n1, 8), n1)

    def rows2(t, c):
        return pl.ds(pl.multiple_of(NU + (2 * t + c) * n2, 8), n2)

    first = [
        send(part.at[:, rows1(t, 1 - core), :], mate1.at[t], m1s.at[t], m1r.at[t], panel=mate)
        for t in range(chips)
    ]
    second = [
        send(part.at[:, rows2(t, 1 - core), NU:], mate2.at[t], m2s.at[t], m2r.at[t], panel=mate)
        for t in range(chips)
    ]
    for p in range(par_dev):
        mirror(p, 0)
    for copy in first:
        copy.start()
    for p in range(par_dev):
        for i in range(1, tiles):
            mirror(p, i)
    for copy in second:
        copy.start()
    others = [lax.rem(chip + j, chips) for j in range(1, chips)]

    def spread(acc, land, ssem, rsem):
        return [
            send(acc.at[o], land.at[j], ssem.at[j], rsem.at[j], panel=2 * o + core)
            for j, o in enumerate(others)
        ]

    def gathered(ref, ssem, rsem, source):
        return [
            send(
                ref.at[at], ref.at[at], ssem.at[j - 1], rsem.at[j - 1],
                panel=lax.rem(own + j, panels),
            )
            for j, at in ((j, source(j)) for j in range(1, panels))
        ]

    def summed(acc, land):
        total = acc[chip]
        for j in range(chips - 1):
            total = total + land[j]
        return total

    for t in range(chips):
        first[t].wait_recv()
        acc0[t] = part[:, rows1(t, core), :NU] + mate1[t, :, :, :NU]
    out0 = spread(acc0, in0, d0s, d0r)
    for copy in out0:
        copy.start()
    for t in range(chips):
        acc1[t] = part[:, rows1(t, core), NU:] + mate1[t, :, :, NU:]
    out1 = spread(acc1, in1, d1s, d1r)
    for copy in out1:
        copy.start()
    for copy in out0:
        copy.wait_recv()
    h0[own] = summed(acc0, in0)
    share0 = gathered(h0, g0s, g0r, lambda j: own)
    for copy in share0:
        copy.start()
    for t in range(chips):
        second[t].wait_recv()
        acc2[t] = part[:, rows2(t, core), NU:] + mate2[t]
    for copy in out1:
        copy.wait_recv()
    h1[own] = summed(acc1, in1)
    share1 = gathered(h1, g1s, g1r, lambda j: own)
    for copy in share1:
        copy.start()
    out2 = spread(acc2, in2, d2s, d2r)
    for copy in out2:
        copy.start()
    for copy in gathered(h0, g0s, g0r, lambda j: lax.rem(own + panels - j, panels)):
        copy.wait_recv()

    row = lax.broadcasted_iota(jnp.int32, (NU, NU), 0)
    col = lax.broadcasted_iota(jnp.int32, (NU, NU), 1)
    mats = []
    for p in range(par_dev):
        mat = jnp.concatenate([h0[q, p] for q in range(panels)], axis=0)
        mats.append(mat + jnp.where(row == col, weight_ref[p : p + 1, :NU], 0.0))
    mats = sweep(tuple(mats), 0, NU // 16)
    for p in range(par_dev):
        inv_ref[p] = mats[p]
    for copy in gathered(h1, g1s, g1r, lambda j: lax.rem(own + panels - j, panels)):
        copy.wait_recv()
    width = order - NU
    on_diag = lax.broadcasted_iota(jnp.int32, (n2, width), 1) == (
        lax.broadcasted_iota(jnp.int32, (n2, width), 0) + own * n2
    )
    pick = jnp.where(on_diag, 1.0, 0.0)
    product = functools.partial(
        lax.dot_general, precision=HI, preferred_element_type=jnp.float32
    )
    taken = []
    for p in range(par_dev):
        cross = jnp.concatenate([h1[q, p] for q in range(panels)], axis=0)
        own_rows = inv_ref[p, pl.ds(pl.multiple_of(own * n1, 8), n1), :]
        gain_ref[p] = -product(own_rows, cross, (((1,), (0,)), ((), ())))
        own_cross = product(pick, cross, (((1,), (1,)), ((), ())))
        lead = product(own_cross, inv_ref[p], (((1,), (0,)), ((), ())))
        taken.append(product(lead, cross, (((1,), (0,)), ((), ()))))
    for copy in out2:
        copy.wait_recv()
    for p in range(par_dev):
        total = acc2[chip, p]
        for j in range(chips - 1):
            total = total + in2[j, p]
        cost_ref[p] = (
            total + jnp.where(on_diag, weight_ref[p : p + 1, NU:], 0.0) - taken[p]
        )
    for copy in first + second + out0 + out1 + out2 + share0 + share1:
        copy.wait_send()

    @pl.loop(1, leaves)
    def _(j):
        piece(j, leaf).wait_send()
        for p in range(par_dev):
            parcel(p, j, leaf).wait_send()

    for j in range(1, panels):
        for p in range(par_dev):
            slot(p, j, own).wait_send()


def level(child_cost, panel, section_weight, parent_slots, child_count, leaves, panels):
    stored, row_block, order = child_cost.shape
    parents, slot_count = parent_slots.shape
    par_dev = parents // leaves
    chips = panels // 2
    half = row_block // 2
    rows = stored * 5 // 2
    groups = slot_count * 5 // 8
    n1, n2 = NU // panels, (order - NU) // panels
    zero, one, two = (par_dev, n1, NU), (par_dev, n1, order - NU), (par_dev, n2, order - NU)
    vmem = pl.BlockSpec(memory_space=pltpu.VMEM)
    smem = pl.BlockSpec(memory_space=pltpu.SMEM)
    hbm = pl.BlockSpec(memory_space=pltpu.HBM)
    dma = pltpu.SemaphoreType.DMA
    word = lambda *shape: pltpu.VMEM(shape + (128,), jnp.int32)
    f32 = lambda *shape: pltpu.VMEM(shape, jnp.float32)
    b16 = lambda *shape: pltpu.VMEM(shape, jnp.bfloat16)
    return pl.pallas_call(
        functools.partial(level_kernel, leaves, panels),
        out_shape=(
            jax.ShapeDtypeStruct((par_dev, n2, order - NU), jnp.float32),
            jax.ShapeDtypeStruct((par_dev, n1, order - NU), jnp.float32),
        ),
        in_specs=[smem, smem, hbm, hbm, vmem],
        out_specs=(vmem, vmem),
        scratch_shapes=[
            f32(stored, row_block, order),
            b16(par_dev, order, order),
            word(leaves * rows),
            word(leaves * rows),
            word(par_dev, leaves, groups, 4),
            word(par_dev, leaves, groups, 4),
            word(par_dev * slot_count * 3 * half),
            word(par_dev, panels, 3 * half),
            b16(par_dev, 2 * order, order),
            b16(par_dev, order, order),
            b16(par_dev, order, order),
            f32(par_dev, order, order),
            f32(par_dev, order, order),
            f32(chips, par_dev, n1, order),
            f32(chips, *two),
            f32(panels, *zero),
            f32(panels, *one),
            f32(chips, *zero),
            f32(chips, *one),
            f32(chips, *two),
            f32(chips - 1, *zero),
            f32(chips - 1, *one),
            f32(chips - 1, *two),
            f32(par_dev, NU, NU),
            dma((stored // 2,)),
            dma,
        ]
        + [dma((leaves - 1,))] * 2
        + [dma((par_dev, leaves - 1))] * 2
        + [dma((par_dev, panels - 1))] * 2
        + [dma((chips,))] * 4
        + [dma((chips - 1,))] * 6
        + [dma((panels - 1,))] * 4,
        compiler_params=pltpu.CompilerParams(
            collective_id=0, has_side_effects=True, vmem_limit_bytes=56 << 20
        ),
        name="level",
    )(parent_slots.T, child_count, child_cost, panel, section_weight)


def store_kernel(cost_ref, gain_ref, cost_out, gain_out, sems):
    copies = [
        pltpu.make_async_copy(cost_ref, cost_out, sems.at[0]),
        pltpu.make_async_copy(gain_ref, gain_out, sems.at[1]),
    ]
    for copy in copies:
        copy.start()
    for copy in copies:
        copy.wait()


def store(cost, gain):
    vmem = pl.BlockSpec(memory_space=pltpu.VMEM)
    hbm = pl.BlockSpec(memory_space=pltpu.HBM)
    return pl.pallas_call(
        store_kernel,
        out_shape=tuple(jax.ShapeDtypeStruct(x.shape, x.dtype) for x in (cost, gain)),
        in_specs=[vmem, vmem],
        out_specs=(hbm, hbm),
        scratch_shapes=[pltpu.SemaphoreType.DMA((2,))],
        name="store",
    )(cost, gain)


def per_device(child_cost, panel, section_weight, parent_slots, child_count):
    leaves = lax.axis_size("leaf")
    panels = lax.axis_size("panel")
    results = level(child_cost, panel, section_weight, parent_slots, child_count, leaves, panels)
    return store(*results)


def solution(mesh):
    in_specs = (P("leaf", "panel", None), P("leaf", "panel", None), P("leaf", None), P(), P())
    out_specs = (P("leaf", "panel", None), P("leaf", "panel", None))
    return jax.shard_map(
        per_device, mesh=mesh, in_specs=in_specs, out_specs=out_specs, check_vma=False
    )
```

```python
import functools

import jax
import jax.numpy as jnp
from jax import lax
from jax.experimental import pallas as pl
from jax.experimental.pallas import tpu as pltpu
from jax.sharding import PartitionSpec as P

NU = 128
HI = lax.Precision.HIGHEST


def pivots(cols, sub):
    for k in range(8):
        inv = 1.0 / jnp.broadcast_to(cols[k][k : k + 1, :], (8, 128))
        rows = [inv if j == k else c[k : k + 1, :] * inv for j, c in enumerate(cols)]
        pivot = cols[k]
        cols = [
            jnp.where(sub == k, rows[j], (0.0 if j == k else c) - pivot * rows[j])
            for j, c in enumerate(cols)
        ]
    return cols


def eight(top, other, at, lane, sub):
    cols = [jnp.broadcast_to(top[:, at + j : at + j + 1], (8, 128)) for j in range(8)]
    cols = pivots(cols, sub)
    new = cols[0] * top[0:1, :]
    for j in range(1, 8):
        new = new + cols[j] * top[j : j + 1, :]
    for j in range(8):
        new = jnp.where(lane == at + j, cols[j], new)
    rest = jnp.where((lane >= at) & (lane < at + 8), 0.0, other)
    for j in range(8):
        rest = rest - other[:, at + j : at + j + 1] * new[j : j + 1, :]
    return new, rest


def sweep(mats, start, stop):
    lane = lax.broadcasted_iota(jnp.int32, (8, 128), 1)
    sub = lax.broadcasted_iota(jnp.int32, (8, 128), 0)
    wide = lax.broadcasted_iota(jnp.int32, (NU - 16, 128), 1)

    def body(_, carry):
        out = []
        for mat in carry:
            one, two = eight(mat[:8], mat[8:16], 0, lane, sub)
            two, one = eight(two, one, 8, lane, sub)
            top = jnp.concatenate([one, two], axis=0)
            rest = mat[16:]
            new = jnp.where(wide < 16, 0.0, rest) - jnp.dot(
                rest[:, :16], top, precision=HI, preferred_element_type=jnp.float32
            )
            out.append(pltpu.roll(jnp.concatenate([new, top], axis=0), 112, 1))
        return tuple(out)

    return lax.fori_loop(start, stop, body, mats)


CODE = 32767.0
STEPS = 64.0


def level_kernel(
    leaves, panels, slots_ref, count_ref, child_hbm, panel_hbm, weight_ref, cost_ref, gain_ref,
    child_ref, a_ref, send1, held, send2, mine, ready, land, t_ref,
    high, low, half_sum, part, mate1, mate2, h0, h1, acc0, acc1, acc2, in0, in1, in2, inv_ref,
    ls, lp, as_, ar, cs, cr, es, er,
    m1s, m1r, m2s, m2r, d0s, d0r, d1s, d1r, d2s, d2r, g0s, g0r, g1s, g1r,
):
    leaf = lax.axis_index("leaf")
    own = lax.axis_index("panel")
    stored, row_block, order = child_ref.shape
    par_dev, _, groups = send2.shape[:3]
    slot_count = slots_ref.shape[0]
    chips = panels // 2
    n1, n2 = gain_ref.shape[1], cost_ref.shape[1]
    tiles = order // 128
    half = row_block // 2
    parts = order // 128
    lane = lax.broadcasted_iota(jnp.int32, (1, 128), 1)
    left = lane < 64
    span = held.shape[0] // leaves
    deep = 5 * half // 2

    def offset(j):
        step = (j + 1) // 2
        return step + (leaves - 2 * step) * (1 - lax.rem(j, 2))

    def send(src, dst, ssem, rsem, **to):
        return pltpu.make_async_remote_copy(
            src_ref=src, dst_ref=dst, send_sem=ssem, recv_sem=rsem,
            device_id=to, device_id_type=pl.DeviceIdType.MESH,
        )

    pairs = stored // 2
    loads = [
        pltpu.make_async_copy(child_hbm.at[pl.ds(2 * n, 2)], child_ref.at[pl.ds(2 * n, 2)], ls.at[n])
        for n in range(pairs)
    ]
    load_panel = pltpu.make_async_copy(panel_hbm, a_ref, lp)
    barrier = pltpu.get_barrier_semaphore()

    @pl.loop(1, leaves)
    def _(j):
        pl.semaphore_signal(
            barrier, inc=1, device_id={"leaf": lax.rem(leaf + j, leaves)},
            device_id_type=pl.DeviceIdType.MESH,
        )

    for j in range(1, panels):
        pl.semaphore_signal(
            barrier, inc=1, device_id={"panel": lax.rem(own + j, panels)},
            device_id_type=pl.DeviceIdType.MESH,
        )

    for copy in loads:
        copy.start()
    load_panel.start()

    chip, core = own // 2, own % 2
    upper = chip // (parts // 2)
    side = core + upper - 2 * core * upper

    word_row = lax.broadcasted_iota(jnp.int32, (half, 128), 0)
    word_lane = lax.broadcasted_iota(jnp.int32, (half, 128), 1)
    scale_at = (word_row == 1) & (word_lane == 64 * core)

    def encode(c):
        cols = [pl.ds(pl.multiple_of(lax.rem(chip + t, parts) * 128, 128), 128) for t in range(3)]
        blocks = [child_ref[c, :, at] for at in cols]
        tops = [jnp.max(jnp.abs(x), keepdims=True) for x in blocks]
        top = jnp.maximum(jnp.maximum(tops[0], tops[1]), jnp.maximum(tops[2], 1e-30))
        mark = jnp.floor(jnp.log2(top) * STEPS) + 1.0
        inv = 1.0 / jnp.exp2(mark * (1.0 / STEPS))
        words = []
        for x in blocks:
            x = x * inv
            size = (jnp.sqrt(jnp.abs(x)) * CODE + 0.5).astype(jnp.int32)
            code = jnp.where(x < 0, -size, size)
            words.append(code[:half] * 65536 + (code[half:] & 65535))
        words[0] = jnp.where(scale_at, mark.astype(jnp.int32), words[0])
        for t in range(2):
            send1[pl.ds(t * stored + c, half, stride=span), :] = words[t]
        return words[2]

    @pl.loop(0, pairs)
    def _(n):
        pltpu.make_async_copy(
            child_hbm.at[pl.ds(2 * n, 2)], child_ref.at[pl.ds(2 * n, 2)], ls.at[n]
        ).wait()
        even, odd = encode(2 * n), encode(2 * n + 1)
        even = jnp.where(side == 0, even, pltpu.roll(even, 64, 1))
        odd = jnp.where(side == 1, odd, pltpu.roll(odd, 64, 1))
        send1[pl.ds(2 * stored + n, half, stride=span), :] = jnp.where(left, even, odd)

    pl.semaphore_wait(barrier, leaves + panels - 2)

    def message(i):
        return pl.ds(pl.multiple_of(i * span, 8), span)

    def piece(j, source):
        to = lax.rem(leaf + offset(j), leaves)
        return send(
            send1.at[message(to)], held.at[message(source)],
            as_.at[j - 1], ar.at[j - 1], leaf=to,
        )

    def source_of(j):
        return lax.rem(leaf + leaves - offset(j), leaves)

    @pl.loop(1, leaves)
    def _(j):
        piece(j, leaf).start()

    held[message(leaf), :] = send1[message(leaf), :]

    @pl.loop(1, leaves)
    def _(j):
        piece(j, source_of(j)).wait_recv()

    def parcel(p, j, source):
        to = lax.rem(leaf + offset(j), leaves)
        return send(
            send2.at[p, to], mine.at[p, source], cs.at[p, j - 1], cr.at[p, j - 1], leaf=to
        )

    def collect(p, d):
        children = [slots_ref[k, d * par_dev + p] for k in range(slot_count)]
        firsts = [lax.shift_right_logical(c, 4) * span for c in children]
        locals_ = [c & (stored - 1) for c in children]
        for t in range(2):
            for k in range(slot_count):
                row = held[pl.ds(firsts[k] + locals_[k] + t * stored, 1), :]
                at = t * slot_count + k
                send2[p, d, at // 4, at % 4 : at % 4 + 1, :] = row
        for n in range(slot_count // 2):
            pick = []
            for e in range(2):
                k = 2 * n + e
                row = held[
                    pl.ds(firsts[k] + 2 * stored + lax.shift_right_logical(locals_[k], 1), 1), :
                ]
                pick.append(jnp.where((locals_[k] & 1) == e, row, pltpu.roll(row, 64, 1)))
            at = 2 * slot_count + n
            send2[p, d, at // 4, at % 4 : at % 4 + 1, :] = jnp.where(left, pick[0], pick[1])

    for p in range(par_dev):

        @pl.loop(1, leaves)
        def _(j):
            collect(p, lax.rem(leaf + offset(j), leaves))
            parcel(p, j, leaf).start()

        collect(p, leaf)
        mine[p, leaf] = send2[p, leaf]

    def slot(p, j, source):
        to = lax.rem(own + j, panels)
        at = pl.ds(pl.multiple_of((p * slot_count + to) * deep, 8), deep)
        return send(
            ready.at[at], land.at[p, source], es.at[p, j - 1], er.at[p, j - 1], panel=to
        )

    def from_of(j):
        return lax.rem(own + panels - j, panels)

    for p in range(par_dev):

        @pl.loop(1, leaves)
        def _(j):
            parcel(p, j, source_of(j)).wait_recv()

        @pl.loop(0, leaves)
        def _(i):
            base = p * slot_count * deep + i
            for t in range(2):
                for g in range(slot_count // 4):
                    at = base + g * 4 * deep + t * half
                    ready[pl.ds(at, 4, stride=deep), :] = mine[p, i, t * slot_count // 4 + g]

        @pl.loop(0, half // 2)
        def _(i):
            base = p * slot_count * deep + 2 * half + i
            for g in range(slot_count // 8):
                one = mine[p, i, slot_count // 2 + g]
                two = mine[p, i + half // 2, slot_count // 2 + g]
                for e in range(2):
                    at = base + (g * 8 + e) * deep
                    ready[pl.ds(at, 4, stride=2 * deep), :] = (
                        jnp.where(left, one, pltpu.roll(two, 64, 1))
                        if e == 0
                        else jnp.where(left, pltpu.roll(one, 64, 1), two)
                    )

        for j in range(1, panels):
            slot(p, j, own).start()
        land[p, own] = ready[
            pl.ds(pl.multiple_of((p * slot_count + own) * deep, 8), deep), :
        ]

    def weights(n, q):
        first_lane = 64 * (q % 2)
        gain = jnp.where((word_row == 1) & (word_lane == first_lane), 0.0, 0.5)
        if n == 0:
            lone = (word_lane == first_lane + 1) | (word_lane == first_lane + 1 + half)
            gain = jnp.where((word_row == 0) & lone, 1.0, gain)
        return gain

    factor = [[weights(n, q) for n in range(2)] for q in range(2)]

    def decode(p, q):
        mark = land[p, q, 1:2, 64 * (q % 2) : 64 * (q % 2) + 1].astype(jnp.float32)
        scale = jnp.exp2(mark * (1.0 / STEPS)) * (1.0 / (CODE * CODE))
        scale = jnp.where(own < count_ref[leaf * par_dev + p], scale, 0.0)
        for t in range(4):
            for n in range(2):
                if t < 3:
                    q_side = (q % 2) ^ (q // 2 // (parts // 2))
                    if t < 2:
                        word = land[p, q, t * half : t * half + half, :]
                    else:
                        packed = land[p, q, 2 * half : deep, :]
                        turned = pltpu.roll(packed, 64, 1)
                        pair = [turned, packed] if q_side else [packed, turned]
                        word = jnp.concatenate(pair, axis=0)
                    code = word >> 16 if n == 0 else (word << 16) >> 16
                    v = code.astype(jnp.float32)
                    v = v * jnp.abs(v) * scale
                    if t == 0:
                        v = v * factor[q % 2][n]
                    if t == 2:
                        v = jnp.where(left if q_side == 0 else ~left, v, 0.0)
                    hi = v.astype(jnp.bfloat16)
                    lo = (v - hi.astype(jnp.float32)).astype(jnp.bfloat16)
                else:
                    hi = lo = jnp.zeros((half, 128), jnp.bfloat16)
                at = (q // 2 + t) % parts * 128
                row = q * row_block + n * half
                t_ref[p, row : row + half, at : at + 128] = hi
                t_ref[p, order + row : order + row + half, at : at + 128] = lo

    load_panel.wait()
    for p in range(par_dev):
        for j in range(1, panels):
            slot(p, j, from_of(j)).wait_recv()
        for q in range(panels):
            decode(p, q)

        @pl.loop(0, tiles)
        def _(i):
            rows = pl.ds(pl.multiple_of(i * 128, 128), 128)
            low_rows = pl.ds(pl.multiple_of(order + i * 128, 128), 128)
            a = a_ref[p]
            prod = jnp.dot(t_ref[p, rows, :], a, preferred_element_type=jnp.float32)
            prod = prod + jnp.dot(t_ref[p, low_rows, :], a, preferred_element_type=jnp.float32)
            top = prod.astype(jnp.bfloat16)
            high[p, rows, :] = top
            low[p, rows, :] = (prod - top.astype(jnp.float32)).astype(jnp.bfloat16)

        @pl.loop(0, tiles)
        def _(i):
            rows = pl.ds(pl.multiple_of(i * 128, 128), 128)
            a = a_ref[p, :, rows]
            total = [
                lax.dot_general(
                    a, x[p], (((0,), (0,)), ((), ())), preferred_element_type=jnp.float32
                )
                for x in (high, low)
            ]
            half_sum[p, rows, :] = total[0] + total[1]

    mate = 2 * chip + 1 - core

    def mirror(p, i):
        rows = slice(i * 128, i * 128 + 128)
        for j in range(tiles):
            cols = slice(j * 128, j * 128 + 128)
            part[p, rows, cols] = half_sum[p, rows, cols] + half_sum[p, cols, rows].T

    def rows1(t, c):
        return pl.ds(pl.multiple_of((2 * t + c) * n1, 8), n1)

    def rows2(t, c):
        return pl.ds(pl.multiple_of(NU + (2 * t + c) * n2, 8), n2)

    first = [
        send(part.at[:, rows1(t, 1 - core), :], mate1.at[t], m1s.at[t], m1r.at[t], panel=mate)
        for t in range(chips)
    ]
    second = [
        send(part.at[:, rows2(t, 1 - core), NU:], mate2.at[t], m2s.at[t], m2r.at[t], panel=mate)
        for t in range(chips)
    ]
    for p in range(par_dev):
        mirror(p, 0)
    for copy in first:
        copy.start()
    for p in range(par_dev):
        for i in range(1, tiles):
            mirror(p, i)
    for copy in second:
        copy.start()
    others = [lax.rem(chip + j, chips) for j in range(1, chips)]

    def spread(acc, land, ssem, rsem):
        return [
            send(acc.at[o], land.at[j], ssem.at[j], rsem.at[j], panel=2 * o + core)
            for j, o in enumerate(others)
        ]

    def gathered(ref, ssem, rsem, source):
        return [
            send(
                ref.at[at], ref.at[at], ssem.at[j - 1], rsem.at[j - 1],
                panel=lax.rem(own + j, panels),
            )
            for j, at in ((j, source(j)) for j in range(1, panels))
        ]

    def summed(acc, land):
        total = acc[chip]
        for j in range(chips - 1):
            total = total + land[j]
        return total

    for t in range(chips):
        first[t].wait_recv()
        acc0[t] = part[:, rows1(t, core), :NU] + mate1[t, :, :, :NU]
    out0 = spread(acc0, in0, d0s, d0r)
    for copy in out0:
        copy.start()
    for t in range(chips):
        acc1[t] = part[:, rows1(t, core), NU:] + mate1[t, :, :, NU:]
    out1 = spread(acc1, in1, d1s, d1r)
    for copy in out1:
        copy.start()
    for copy in out0:
        copy.wait_recv()
    h0[own] = summed(acc0, in0)
    share0 = gathered(h0, g0s, g0r, lambda j: own)
    for copy in share0:
        copy.start()
    for t in range(chips):
        second[t].wait_recv()
        acc2[t] = part[:, rows2(t, core), NU:] + mate2[t]
    for copy in out1:
        copy.wait_recv()
    h1[own] = summed(acc1, in1)
    share1 = gathered(h1, g1s, g1r, lambda j: own)
    for copy in share1:
        copy.start()
    out2 = spread(acc2, in2, d2s, d2r)
    for copy in out2:
        copy.start()
    for copy in gathered(h0, g0s, g0r, lambda j: lax.rem(own + panels - j, panels)):
        copy.wait_recv()

    row = lax.broadcasted_iota(jnp.int32, (NU, NU), 0)
    col = lax.broadcasted_iota(jnp.int32, (NU, NU), 1)
    mats = []
    for p in range(par_dev):
        mat = jnp.concatenate([h0[q, p] for q in range(panels)], axis=0)
        mats.append(mat + jnp.where(row == col, weight_ref[p : p + 1, :NU], 0.0))
    mats = sweep(tuple(mats), 0, NU // 16)
    for p in range(par_dev):
        inv_ref[p] = mats[p]
    for copy in gathered(h1, g1s, g1r, lambda j: lax.rem(own + panels - j, panels)):
        copy.wait_recv()
    width = order - NU
    on_diag = lax.broadcasted_iota(jnp.int32, (n2, width), 1) == (
        lax.broadcasted_iota(jnp.int32, (n2, width), 0) + own * n2
    )
    pick = jnp.where(on_diag, 1.0, 0.0)
    product = functools.partial(
        lax.dot_general, precision=HI, preferred_element_type=jnp.float32
    )
    taken = []
    for p in range(par_dev):
        cross = jnp.concatenate([h1[q, p] for q in range(panels)], axis=0)
        own_rows = inv_ref[p, pl.ds(pl.multiple_of(own * n1, 8), n1), :]
        gain_ref[p] = -product(own_rows, cross, (((1,), (0,)), ((), ())))
        own_cross = product(pick, cross, (((1,), (1,)), ((), ())))
        lead = product(own_cross, inv_ref[p], (((1,), (0,)), ((), ())))
        taken.append(product(lead, cross, (((1,), (0,)), ((), ()))))
    for copy in out2:
        copy.wait_recv()
    for p in range(par_dev):
        total = acc2[chip, p]
        for j in range(chips - 1):
            total = total + in2[j, p]
        cost_ref[p] = (
            total + jnp.where(on_diag, weight_ref[p : p + 1, NU:], 0.0) - taken[p]
        )
    for copy in first + second + out0 + out1 + out2 + share0 + share1:
        copy.wait_send()

    @pl.loop(1, leaves)
    def _(j):
        piece(j, leaf).wait_send()
        for p in range(par_dev):
            parcel(p, j, leaf).wait_send()

    for j in range(1, panels):
        for p in range(par_dev):
            slot(p, j, own).wait_send()


def level(child_cost, panel, section_weight, parent_slots, child_count, leaves, panels):
    stored, row_block, order = child_cost.shape
    parents, slot_count = parent_slots.shape
    par_dev = parents // leaves
    chips = panels // 2
    half = row_block // 2
    rows = stored * 5 // 2
    groups = slot_count * 5 // 8
    n1, n2 = NU // panels, (order - NU) // panels
    zero, one, two = (par_dev, n1, NU), (par_dev, n1, order - NU), (par_dev, n2, order - NU)
    vmem = pl.BlockSpec(memory_space=pltpu.VMEM)
    smem = pl.BlockSpec(memory_space=pltpu.SMEM)
    hbm = pl.BlockSpec(memory_space=pltpu.HBM)
    dma = pltpu.SemaphoreType.DMA
    word = lambda *shape: pltpu.VMEM(shape + (128,), jnp.int32)
    f32 = lambda *shape: pltpu.VMEM(shape, jnp.float32)
    b16 = lambda *shape: pltpu.VMEM(shape, jnp.bfloat16)
    return pl.pallas_call(
        functools.partial(level_kernel, leaves, panels),
        out_shape=(
            jax.ShapeDtypeStruct((par_dev, n2, order - NU), jnp.float32),
            jax.ShapeDtypeStruct((par_dev, n1, order - NU), jnp.float32),
        ),
        in_specs=[smem, smem, hbm, hbm, vmem],
        out_specs=(vmem, vmem),
        scratch_shapes=[
            f32(stored, row_block, order),
            b16(par_dev, order, order),
            word(leaves * rows),
            word(leaves * rows),
            word(par_dev, leaves, groups, 4),
            word(par_dev, leaves, groups, 4),
            word(par_dev * slot_count * 5 * half // 2),
            word(par_dev, panels, 5 * half // 2),
            b16(par_dev, 2 * order, order),
            b16(par_dev, order, order),
            b16(par_dev, order, order),
            f32(par_dev, order, order),
            f32(par_dev, order, order),
            f32(chips, par_dev, n1, order),
            f32(chips, *two),
            f32(panels, *zero),
            f32(panels, *one),
            f32(chips, *zero),
            f32(chips, *one),
            f32(chips, *two),
            f32(chips - 1, *zero),
            f32(chips - 1, *one),
            f32(chips - 1, *two),
            f32(par_dev, NU, NU),
            dma((stored // 2,)),
            dma,
        ]
        + [dma((leaves - 1,))] * 2
        + [dma((par_dev, leaves - 1))] * 2
        + [dma((par_dev, panels - 1))] * 2
        + [dma((chips,))] * 4
        + [dma((chips - 1,))] * 6
        + [dma((panels - 1,))] * 4,
        compiler_params=pltpu.CompilerParams(
            collective_id=0, has_side_effects=True, vmem_limit_bytes=56 << 20
        ),
        name="level",
    )(parent_slots.T, child_count, child_cost, panel, section_weight)


def store_kernel(cost_ref, gain_ref, cost_out, gain_out, sems):
    copies = [
        pltpu.make_async_copy(cost_ref, cost_out, sems.at[0]),
        pltpu.make_async_copy(gain_ref, gain_out, sems.at[1]),
    ]
    for copy in copies:
        copy.start()
    for copy in copies:
        copy.wait()


def store(cost, gain):
    vmem = pl.BlockSpec(memory_space=pltpu.VMEM)
    hbm = pl.BlockSpec(memory_space=pltpu.HBM)
    return pl.pallas_call(
        store_kernel,
        out_shape=tuple(jax.ShapeDtypeStruct(x.shape, x.dtype) for x in (cost, gain)),
        in_specs=[vmem, vmem],
        out_specs=(hbm, hbm),
        scratch_shapes=[pltpu.SemaphoreType.DMA((2,))],
        name="store",
    )(cost, gain)


def per_device(child_cost, panel, section_weight, parent_slots, child_count):
    leaves = lax.axis_size("leaf")
    panels = lax.axis_size("panel")
    results = level(child_cost, panel, section_weight, parent_slots, child_count, leaves, panels)
    return store(*results)


def solution(mesh):
    in_specs = (P("leaf", "panel", None), P("leaf", "panel", None), P("leaf", None), P(), P())
    out_specs = (P("leaf", "panel", None), P("leaf", "panel", None))
    return jax.shard_map(
        per_device, mesh=mesh, in_specs=in_specs, out_specs=out_specs, check_vma=False
    )
```
